32 devices in a mesh: case: 2 (over x), span: 8 (over z, y), dom: 2 (over core).
Axes of the slice: x: 2, y: 2, z: 4, core: 2. Of those that a mesh axis runs over, the one named last changes fastest.
Arguments:
- scalar: float32 [256, 8192], P(('case', 'span'), 'dom'), parts along dimension 0, may hold values from -6 to 6
- span_vel: float32 [256, 8192], P(('case', 'span'), 'dom'), parts along dimension 0, may hold values from -4 to 4
- flux_weight: float32 [4, 8192], P(None, 'dom'), may hold values from -4 to 4
- neighbours: int32 [4, 8192], P(None, 'dom'), may hold values from 0 to 8191, as said below
- diagonal: float32 [8192], P('dom'), may hold values from 0.5 to 2
- interface: int32 [16, 128], P('dom'), may hold values from 0 to 8191, as said below
- schur_one: float32 [128, 8, 128, 128], P('span', 'dom'), may hold values from -1 to 1
- schur_two: float32 [128, 4, 128, 128], P('span', 'dom'), may hold values from -1 to 1
- schur_three: float32 [128, 2, 128, 128], P('span', 'dom'), may hold values from -1 to 1
- schur_root: float32 [128, 1, 128, 128], P('span'), may hold values from -1 to 1
Outputs:
- pressure: float32 [256, 8192], P(('case', 'span'), 'dom'), parts along dimension 0
- corrected: float32 [256, 8192], P(('case', 'span'), 'dom'), parts along dimension 0
The draws below stay inside these ranges and needn't reach their ends.
There are 2 independent parts, one for each index of `case`. The reference program is written for one: setup_inputs(seed, part) draws one part's arguments, and reference() takes and returns one part's arrays. A program takes and returns all parts, laid end to end along the dimension named above; an argument that names none is the same for every part. Nothing has to cross between parts.
Inputs may be any that keep to these rules, and one draw needn't show every extreme that they name: `neighbours`: every entry lies 1 to 64 cells from its own cell in the numbering, and the distance 64 occurs. `interface`: row d holds 128 distinct cells of subdomain d, numbered from d * 512 to (d + 1) * 512 - 1.
All inputs are finite; a program needn't handle non-finite values.
Results may differ from the reference program's by a relative error of at most 0.0001.
Values sent between devices are 32-bit elements; how exact they have to be, the bound alone decides.
No kernel may reach another device: no remote copies, remote signals or barrier semaphores. Data moves between devices by JAX's collectives and lax.ppermute only.
A program may use at most 64 MiB of HBM per device.

```python
import math
import jax
import jax.numpy as jnp
from jax import lax

PLANES = 128
DOMAINS = 16
CELL_DOM = 512
B = 128
HALO = 64
NBR = 4
CELLS = 8192


def schur_draw(key, nodes):
    first = jax.random.fold_in(key, 0)
    shape = (PLANES, nodes, B, B)
    identity = jnp.eye(B, dtype=jnp.float32)
    noise = jax.random.normal(first, shape, jnp.float32) * (0.3 / math.sqrt(B))
    return jnp.clip(0.6 * identity + noise, -1.0, 1.0)


def draw_schur_one(key, part):
    return schur_draw(jax.random.fold_in(key, 11), DOMAINS // 2)


def draw_schur_two(key, part):
    return schur_draw(jax.random.fold_in(key, 12), DOMAINS // 4)


def draw_schur_three(key, part):
    return schur_draw(jax.random.fold_in(key, 13), DOMAINS // 8)


def draw_schur_root(key, part):
    return schur_draw(jax.random.fold_in(key, 14), 1)


def draw_neighbours(key, part):
    first, second = jax.random.split(jax.random.fold_in(key, 21))
    cell_ids = jnp.arange(CELLS, dtype=jnp.int32)[None, :]
    lengths = jax.random.randint(first, (NBR, CELLS), 1, HALO + 1)
    lengths = jnp.where(cell_ids % 16 == 0, HALO, lengths)
    signs = jax.random.randint(second, (NBR, CELLS), 0, 2) * 2 - 1
    target = cell_ids + signs * lengths
    outside = (target < 0) | (target >= CELLS)
    target = jnp.where(outside, cell_ids - signs * lengths, target)
    return target.astype(jnp.int32)


def draw_interface(key, part):
    domain_keys = jax.random.split(jax.random.fold_in(key, 31), DOMAINS)
    chosen = jax.vmap(lambda single: jax.random.permutation(single, CELL_DOM)[:B])(domain_keys)
    offsets = jnp.arange(DOMAINS, dtype=jnp.int32)[:, None] * CELL_DOM
    return (chosen + offsets).astype(jnp.int32)


def steps_of(own_key, dims, shards, least, high):
    def one(dim, parts):
        draws = jax.random.uniform(jax.random.fold_in(jax.random.fold_in(own_key, 6), dim), (parts,), jnp.float32, least / len(shards), high / len(shards))
        return jnp.repeat(jnp.exp(draws), dims[dim] // parts).reshape((-1,) + (1,) * (len(dims) - dim - 1))

    loudness = one(*shards[0])
    for cut in shards[1:]:
        loudness = loudness * one(*cut)
    return loudness


def scatter_about(own_key, dims, spread, bound, cuts=(), kind=jnp.bfloat16):
    result = jax.random.normal(own_key, dims, jnp.float32) * spread
    if len(cuts) > 0:
        result = steps_of(own_key, dims, cuts, -0.22, 0.18) * result
    return jnp.clip(result, min=-bound, max=bound).astype(kind)


def setup_inputs(seed: int = 0, part: int = 0) -> dict:
    arg_keys = jax.random.split(jax.random.key(seed), 11)
    part_keys = jax.random.split(jax.random.fold_in(arg_keys[10], part), 11)
    scalar = scatter_about(part_keys[0], (PLANES, CELLS), 1.0, 6.0, ((0, 8), (1, 2)), jnp.float32)
    span_vel = scatter_about(part_keys[1], (PLANES, CELLS), 0.5, 4.0, ((0, 8), (1, 2)), jnp.float32)
    flux_weight = scatter_about(arg_keys[2], (NBR, CELLS), 0.5, 4.0, ((1, 2),), jnp.float32)
    neighbours = draw_neighbours(jax.random.fold_in(arg_keys[10], 71), part)
    diagonal = jnp.clip(0.5 + 1.5 * jax.random.uniform(arg_keys[4], (CELLS,), jnp.float32) ** steps_of(arg_keys[4], (CELLS,), ((0, 2),), -0.2, 0.2), 0.5, 2.0)
    interface = draw_interface(jax.random.fold_in(arg_keys[10], 71), part)
    schur_one = draw_schur_one(jax.random.fold_in(arg_keys[10], 71), part)
    schur_two = draw_schur_two(jax.random.fold_in(arg_keys[10], 71), part)
    schur_three = draw_schur_three(jax.random.fold_in(arg_keys[10], 71), part)
    schur_root = draw_schur_root(jax.random.fold_in(arg_keys[10], 71), part)
    return dict(scalar=scalar, span_vel=span_vel, flux_weight=flux_weight, neighbours=neighbours, diagonal=diagonal, interface=interface, schur_one=schur_one, schur_two=schur_two, schur_three=schur_three, schur_root=schur_root)


def fourier_entry(wave_ids, plane_ids):
    middle = PLANES // 2
    wave_num = jnp.where(wave_ids <= middle, wave_ids, wave_ids - middle)
    phase_angle = (wave_num * plane_ids % PLANES).astype(jnp.float32) * (2.0 * math.pi / PLANES)
    at_edge = (wave_ids == 0) | (wave_ids == middle)
    weight_row = jnp.where(at_edge, math.sqrt(1.0 / PLANES), math.sqrt(2.0 / PLANES))
    return jnp.where(wave_ids <= middle, jnp.cos(phase_angle), jnp.sin(phase_angle)) * weight_row

def wave_shift(wave_ids):
    middle = PLANES // 2
    wave_num = jnp.where(wave_ids <= middle, wave_ids, wave_ids - middle).astype(jnp.float32)
    return (2.0 * jnp.sin(wave_num * (math.pi / PLANES))) ** 2

def stencil(field, span_vel, flux_weight, neighbours):
    ahead = jnp.roll(field, -1, 0)
    behind = jnp.roll(field, 1, 0)
    convected = span_vel * 0.5 * (ahead - behind)
    for slot in range(NBR):
        convected = convected + flux_weight[slot] * (field[:, neighbours[slot]] - field)
    return convected

def reference(scalar, span_vel, flux_weight, neighbours, diagonal, interface, schur_one, schur_two, schur_three, schur_root):
    source = scalar - stencil(scalar, span_vel, flux_weight, neighbours)
    wave_ids = jnp.arange(PLANES, dtype=jnp.int32)
    wave_table = fourier_entry(wave_ids[:, None], wave_ids[None, :])
    spectrum = jnp.dot(wave_table, source, precision=lax.Precision.HIGHEST)
    interior = spectrum / (diagonal[None, :] + wave_shift(wave_ids)[:, None])
    leaves = interior[:, interface]
    levels = [leaves]
    current = leaves
    for blocks in (schur_one, schur_two, schur_three):
        paired = current[:, 0::2] + current[:, 1::2]
        current = jnp.einsum('mnij,mnj->mni', blocks, paired, precision=lax.Precision.HIGHEST)
        levels.append(current)
    paired = current[:, 0::2] + current[:, 1::2]
    top_value = jnp.einsum('mnij,mnj->mni', schur_root, paired, precision=lax.Precision.HIGHEST)
    returned = jnp.einsum('mnji,mnj->mni', schur_root, top_value, precision=lax.Precision.HIGHEST)
    lowered = levels[3] - jnp.repeat(returned, 2, axis=1)
    for blocks, below in ((schur_three, levels[2]), (schur_two, levels[1]), (schur_one, levels[0])):
        returned = jnp.einsum('mnji,mnj->mni', blocks, lowered, precision=lax.Precision.HIGHEST)
        lowered = below - jnp.repeat(returned, 2, axis=1)
    corrected_spectrum = interior.at[:, interface].add(-0.5 * lowered)
    pressure = jnp.dot(wave_table.T, corrected_spectrum, precision=lax.Precision.HIGHEST)
    corrected = scalar - stencil(pressure, span_vel, flux_weight, neighbours)
    return (pressure, corrected)
```

```python
import functools
import math

import jax
import jax.numpy as jnp
from jax import lax
from jax.experimental import pallas as pl
from jax.experimental.pallas import tpu as pltpu
from jax.sharding import PartitionSpec as P

PLANES = 128
LANES = 128
SUB = 8
HALF = LANES // 2
F32 = jnp.float32
BF16 = jnp.bfloat16
EXACT = lax.Precision.HIGHEST


def fourier_entry(wave_ids, plane_ids):
    middle = PLANES // 2
    wave_num = jnp.where(wave_ids <= middle, wave_ids, wave_ids - middle)
    phase_angle = (wave_num * plane_ids % PLANES).astype(F32) * (2.0 * math.pi / PLANES)
    at_edge = (wave_ids == 0) | (wave_ids == middle)
    weight_row = jnp.where(at_edge, math.sqrt(1.0 / PLANES), math.sqrt(2.0 / PLANES))
    return jnp.where(wave_ids <= middle, jnp.cos(phase_angle), jnp.sin(phase_angle)) * weight_row


def wave_shift(wave_ids):
    middle = PLANES // 2
    wave_num = jnp.where(wave_ids <= middle, wave_ids, wave_ids - middle).astype(F32)
    return (2.0 * jnp.sin(wave_num * (math.pi / PLANES))) ** 2


def xor_permute(value, axis, mask):
    return lax.ppermute(value, axis, [(i, i ^ mask) for i in range(lax.axis_size(axis))])


def gathered(block, axis):
    count = lax.axis_size(axis)
    far = [xor_permute(block, axis, mask) for mask in range(count - 2, 0, -2)]
    mine = jnp.concatenate([block] + far[::-1], axis=0)
    return mine, xor_permute(mine, axis, 1)


def xor_offsets(count):
    return list(range(0, count, 2)) + list(range(1, count, 2))


def whole(*shapes):
    return [pl.BlockSpec(memory_space=pltpu.VMEM) for _ in shapes]


def lane_take(source, index):
    return jnp.take_along_axis(source, index, axis=1, mode="promise_in_bounds")


def decay(diag):
    root = jnp.sqrt(diag + 0.25 * diag * diag)
    return 1.0 / (1.0 + 0.5 * diag + root), 0.5 / root


def powers(base, exponent, limit):
    result = None
    bit, factor = 1, base
    while bit < limit:
        part = jnp.where((exponent & bit) != 0, factor, 1.0)
        result = part if result is None else result * part
        factor = factor * factor
        bit *= 2
    return result


def convection(ext, block, nblocks, rows, sv, fw_ref, nb_ref):
    start = pl.multiple_of(block * LANES, LANES)
    here = pl.multiple_of(start + LANES, LANES)
    field = ext[pl.ds(SUB, rows), pl.ds(here, LANES)]
    before = ext[pl.ds(SUB, rows), pl.ds(start, LANES)]
    after = ext[pl.ds(SUB, rows), pl.ds(pl.multiple_of(here + LANES, LANES), LANES)]
    lane = lax.broadcasted_iota(jnp.int32, (rows, LANES), 1)
    around = jnp.where(lane < HALF, after, before)
    ahead = ext[pl.ds(SUB + 1, rows), pl.ds(here, LANES)]
    behind = ext[pl.ds(SUB - 1, rows), pl.ds(here, LANES)]
    total = sv * 0.5 * (ahead - behind)
    for slot in range(fw_ref.shape[0]):
        ids = nb_ref[pl.ds(slot, 1), pl.ds(start, LANES)]
        index = jnp.broadcast_to(ids & (LANES - 1), (rows, LANES))
        inside = (((ids >> 7) - block) & (nblocks - 1)) == 0
        near = jnp.where(inside, lane_take(field, index), lane_take(around, index))
        total = total + fw_ref[pl.ds(slot, 1), pl.ds(start, LANES)] * (near - field)
    return field, total


def fill(ext, field_ref, halo_ref, rows, cells):
    ext[pl.ds(SUB, rows), pl.ds(LANES, cells)] = field_ref[...]
    ext[pl.ds(SUB, rows), pl.ds(0, LANES)] = halo_ref[...]
    ext[pl.ds(SUB, rows), pl.ds(LANES + cells, LANES)] = halo_ref[...]


def source_kernel(
    planes, v_ref, halo_ref, sv_ref, fw_ref, nb_ref, diag_ref, iface_ref,
    pay_ref, q_ref, edge_ref, dif_ref, ext, strip,
):
    rows, cells = v_ref.shape
    nblocks = cells // LANES
    fill(ext, v_ref, halo_ref, rows, cells)
    ext[pl.ds(0, SUB), :] = jnp.zeros((SUB, cells + 2 * LANES), F32)
    ext[pl.ds(SUB + rows, SUB), :] = jnp.zeros((SUB, cells + 2 * LANES), F32)
    row = lax.broadcasted_iota(jnp.int32, (rows, LANES), 0)

    def step(block, carry):
        start = pl.multiple_of(block * LANES, LANES)
        sv = sv_ref[:, pl.ds(start, LANES)]
        field, total = convection(ext, block, nblocks, rows, sv, fw_ref, nb_ref)
        source = field - total
        diag = diag_ref[pl.ds(block, 1), :]
        lam, kappa = decay(diag)
        forward, backward, factor, shift = source, source, lam, 1
        while shift < planes:
            down = jnp.where(row >= shift, pltpu.roll(forward, shift, 0), 0.0)
            up = jnp.where(row < rows - shift, pltpu.roll(backward, rows - shift, 0), 0.0)
            forward = forward + factor * down
            backward = backward + factor * up
            factor, shift = factor * factor, shift * 2
        local = kappa * (forward + (backward - source))
        q_ref[:, pl.ds(start, LANES)] = local
        last = planes - 1
        edges = (
            local[0:1], local[last:planes], field[0:1], field[last:planes], sv[0:1], sv[last:planes], diag,
        )
        for place, value in enumerate(edges):
            strip[pl.ds(place, 1), pl.ds(start, LANES)] = value
            if place < 6:
                edge_ref[place, pl.ds(block, 1), :] = value
        return carry

    lax.fori_loop(0, nblocks, step, 0, unroll=2)
    domains = iface_ref.shape[0]
    width = cells // domains
    for pair in range(domains // 2):
        total = None
        for domain in (2 * pair, 2 * pair + 1):
            where = iface_ref[pl.ds(domain, 1), :] & (width - 1)
            lane, which = where & (LANES - 1), where >> 7
            inner = jnp.zeros((rows, LANES), F32)
            outer = jnp.zeros((SUB, LANES), F32)
            for part in range(width // LANES):
                start = domain * width + part * LANES
                here = which == part
                index = jnp.broadcast_to(lane, (rows, LANES))
                inner = jnp.where(here, lane_take(q_ref[:, pl.ds(start, LANES)], index), inner)
                index = jnp.broadcast_to(lane, (SUB, LANES))
                outer = jnp.where(here, lane_take(strip[:, pl.ds(start, LANES)], index), outer)
            total = inner if total is None else total + inner
            for place in range(6):
                at = 2 * rows + SUB * (place // 2) + domain
                pay_ref[pl.ds(at, 1), pl.ds((place % 2) * LANES, LANES)] = outer[place : place + 1]
            dif_ref[pl.ds(domain, 1), :] = outer[6:7]
        half, column = divmod(pair, domains // 4)
        pay_ref[pl.ds(half * rows, rows), pl.ds(column * LANES, LANES)] = total


def slot_kernel(iface_ref, inv_ref):
    domains, slots = iface_ref.shape
    nblocks = inv_ref.shape[0]
    per = nblocks // domains
    columns = jnp.transpose(jnp.concatenate([iface_ref[...].astype(F32)] * (LANES // domains), axis=0))
    lane = lax.broadcasted_iota(jnp.int32, (slots, LANES), 1)
    slot = lax.broadcasted_iota(jnp.int32, (slots, LANES), 0).astype(F32)
    for domain in range(domains):
        own = columns[:, domain : domain + 1].astype(jnp.int32) & (per * LANES - 1)
        own = jnp.broadcast_to(own, (slots, LANES))
        for part in range(per):
            hit = jnp.where(own == lane + part * LANES, slot, -1.0)
            found = jnp.max(hit, axis=0, keepdims=True)
            inv_ref[pl.ds(domain * per + part, 1), :] = found.astype(jnp.int32)


def matvec(vector, matrix, contract):
    high = matrix.astype(BF16)
    low = (matrix - high.astype(F32)).astype(BF16)
    vhigh = vector.astype(BF16).astype(F32)
    vlow = vector - vhigh
    row = lax.broadcasted_iota(jnp.int32, (SUB, LANES), 0)
    first = jnp.where(row == 0, vhigh, 0.0)
    both = jnp.where(row == 1, vlow, first).astype(BF16)
    numbers = (((1,), (contract,)), ((), ()))
    out = lax.dot_general(both, high, numbers, preferred_element_type=F32)
    out = out + lax.dot_general(first.astype(BF16), low, numbers, preferred_element_type=F32)
    return out[0:1] + out[1:2]


def copies(pairs, sems, chunk, size):
    return [
        pltpu.make_async_copy(src.at[pl.ds(chunk * size, size)], dst.at[pl.ds(chunk * size, size)], sems.at[i, chunk])
        for i, (src, dst) in enumerate(pairs)
    ]


def up_kernel(
    offsets, rows, me_ref, mine_ref, recv_ref, table_ref, edge_ref, sigma_ref, dif_ref, m1_hbm, m2_hbm, m3_hbm,
    s3_ref, keep_ref, m1, m2, m3, sems, q, edges, pairs, spectrum,
):
    waves = m1_hbm.shape[0]
    count = len(offsets)
    chunks = sems.shape[1]
    size = waves // chunks
    moved = ((m1_hbm, m1), (m2_hbm, m2), (m3_hbm, m3))
    for chunk in range(chunks):
        for copy in copies(moved, sems, chunk, size):
            copy.start()
    me = me_ref[0]
    block_rows = 2 * rows + 3 * SUB
    for place, offset in enumerate(offsets):
        source = mine_ref if place < count // 2 else recv_ref
        base = (place % (count // 2)) * block_rows
        for half in range(2):
            q[pl.ds(place * rows, rows), pl.ds(half * 2 * LANES, 2 * LANES)] = source[
                pl.ds(base + half * rows, rows), :
            ]
        edges[me ^ offset] = source[pl.ds(base + 2 * rows, 3 * SUB), :]
    wide = jnp.dot(table_ref[...], q[...], precision=EXACT, preferred_element_type=F32)
    for node in range(spectrum.shape[0]):
        spectrum[node] = wide[:, node * LANES : (node + 1) * LANES]
    dif = dif_ref[...]
    lam, _ = decay(dif)
    first_of = lambda t, place: edges[t, pl.ds(SUB * place, SUB), pl.ds(0, LANES)]
    last_of = lambda t, place: edges[t, pl.ds(SUB * place, SUB), pl.ds(LANES, LANES)]
    residual = []
    for t in range(count):
        prev, succ = (t - 1) % count, (t + 1) % count
        residual.append(last_of(prev, 0) - lam * first_of(t, 0) + 0.5 * first_of(t, 2) * last_of(prev, 1))
        residual.append(first_of(succ, 0) - lam * last_of(t, 0) - 0.5 * last_of(t, 2) * first_of(succ, 1))

    def edge_step(wave, carry):
        total = edge_ref[wave, 0] * residual[0]
        for place in range(1, 2 * count):
            total = total + edge_ref[wave, place] * residual[place]
        leaf = total / (dif + sigma_ref[wave])
        pairs[wave] = leaf + pltpu.roll(leaf, SUB - 1, 0)
        return carry

    lax.fori_loop(0, waves, edge_step, 0)

    def chunk_step(chunk, carry):
        for copy in copies(moved, sems, chunk, size):
            copy.wait()
        for inner in range(size):
            wave = chunk * size + inner
            level = [
                spectrum[node, pl.ds(wave, 1), :] + pairs[wave, pl.ds(2 * node, 1), :]
                for node in range(m1.shape[1])
            ]
            at = 0
            for blocks in (m1, m2, m3):
                level = [matvec(vector, blocks[wave, node], 1) for node, vector in enumerate(level)]
                for node, vector in enumerate(level):
                    keep_ref[wave, pl.ds(at + node, 1), :] = vector
                at += len(level)
                if len(level) > 1:
                    level = [level[2 * node] + level[2 * node + 1] for node in range(len(level) // 2)]
            s3_ref[pl.ds(wave, 1), :] = level[0]
        return carry

    lax.fori_loop(0, chunks, chunk_step, 0)


def down_kernel(
    s3_ref, other_ref, keep_ref, root_hbm, m3_hbm, m2_hbm, m1_hbm, out_ref, root, m3, m2, m1, sems
):
    waves = m1_hbm.shape[0]
    chunks = sems.shape[1]
    size = waves // chunks
    moved = ((root_hbm, root), (m3_hbm, m3), (m2_hbm, m2), (m1_hbm, m1))
    for chunk in range(chunks):
        for copy in copies(moved, sems, chunk, size):
            copy.start()
    if out_ref.shape[1] > waves:
        out_ref[...] = jnp.zeros(out_ref.shape, F32)

    def chunk_step(chunk, carry):
        for copy in copies(moved, sems, chunk, size):
            copy.wait()
        for inner in range(size):
            wave = chunk * size + inner
            own = s3_ref[pl.ds(wave, 1), :]
            top = matvec(own + other_ref[pl.ds(wave, 1), :], root[wave, 0], 1)
            lowered = [own - matvec(top, root[wave, 0], 0)]
            at = 2 * m1.shape[1] - 2
            for blocks in (m3, m2, m1):
                returned = [matvec(vector, blocks[wave, node], 0) for node, vector in enumerate(lowered)]
                nodes = 2 * len(returned)
                if nodes > m1.shape[1]:
                    break
                at -= nodes
                lowered = [keep_ref[wave, pl.ds(at + node, 1), :] - returned[node // 2] for node in range(nodes)]
            for node, vector in enumerate(returned):
                out_ref[node, pl.ds(wave, 1), :] = vector
        return carry

    lax.fori_loop(0, chunks, chunk_step, 0)


def pressure_kernel(
    planes, domains, count, mine_ref, recv_ref, table_ref, q_ref, inflow_ref, diag_ref, inv_ref,
    pressure_ref, hal_ref, change, waves,
):
    rows, cells = q_ref.shape
    nblocks = cells // LANES
    per_pair = 2 * nblocks // domains
    wave_rows, nodes = waves.shape[0] // count, waves.shape[1] // LANES
    for place in range(count):
        source = mine_ref if place < count // 2 else recv_ref
        base = (place % (count // 2)) * nodes * wave_rows
        for node in range(nodes):
            waves[pl.ds(place * wave_rows, wave_rows), pl.ds(node * LANES, LANES)] = source[
                pl.ds(base + node * wave_rows, wave_rows), :
            ]
    change[...] = jnp.dot(table_ref[...], waves[...], precision=EXACT, preferred_element_type=F32)
    row = lax.broadcasted_iota(jnp.int32, (rows, LANES), 0)
    edge_row = lax.broadcasted_iota(jnp.int32, (SUB, LANES), 0)

    def step(block, carry):
        start = pl.multiple_of(block * LANES, LANES)
        lam, _ = decay(diag_ref[pl.ds(block, 1), :])
        left, right, at_first, at_last = (inflow_ref[i, pl.ds(block, 1), :] for i in range(4))
        from_left = at_first + lam * left
        from_right = at_last + lam * right
        local = q_ref[:, pl.ds(start, LANES)]
        value = local + powers(lam, row, planes) * from_left + powers(lam, (planes - 1) - row, planes) * from_right
        span = lam
        for _ in range(int(math.log2(planes))):
            span = span * span
        before = lam * local[0:1] + left + lam * at_first + span * from_right
        after = lam * local[planes - 1 : planes] + right + lam * at_last + span * from_left
        outer = jnp.where(edge_row == 0, before, after)
        slot = inv_ref[pl.ds(block, 1), :]
        taken = slot >= 0
        column = pl.multiple_of((block // per_pair) * LANES, LANES)
        source = change[:, pl.ds(column, LANES)]
        got = lane_take(source, jnp.broadcast_to(jnp.maximum(slot, 0), source.shape))
        pressure_ref[:, pl.ds(start, LANES)] = jnp.where(taken, 0.5 * value + 0.5 * got[:rows], value)
        hal_ref[:, pl.ds(start, LANES)] = jnp.where(taken, 0.5 * outer + 0.5 * got[rows:], outer)
        return carry

    lax.fori_loop(0, nblocks, step, 0, unroll=2)


def corrected_kernel(planes, v_ref, p_ref, hal_ref, halo_ref, sv_ref, fw_ref, nb_ref, out_ref, ext):
    rows, cells = v_ref.shape
    nblocks = cells // LANES
    fill(ext, p_ref, halo_ref, rows, cells)
    ext[pl.ds(SUB - 1, 1), pl.ds(LANES, cells)] = hal_ref[pl.ds(0, 1), :]
    ext[pl.ds(SUB + planes, 1), pl.ds(LANES, cells)] = hal_ref[pl.ds(1, 1), :]

    def step(block, carry):
        start = pl.multiple_of(block * LANES, LANES)
        sv = sv_ref[:, pl.ds(start, LANES)]
        _, total = convection(ext, block, nblocks, rows, sv, fw_ref, nb_ref)
        out_ref[:, pl.ds(start, LANES)] = v_ref[:, pl.ds(start, LANES)] - total
        return carry

    lax.fori_loop(0, nblocks, step, 0, unroll=2)


PARAMS = pltpu.CompilerParams(vmem_limit_bytes=40 * 1024 * 1024)


def call(kernel, outs, args, scratch=(), specs=None, name=None):
    return pl.pallas_call(
        kernel,
        out_shape=[jax.ShapeDtypeStruct(*out) for out in outs],
        in_specs=specs or whole(*args),
        out_specs=whole(*outs),
        scratch_shapes=list(scratch),
        compiler_params=PARAMS,
        name=name,
    )(*args)


def inflow(ends, diag, planes):
    count, me = lax.axis_size("span"), lax.axis_index("span")
    lam, _ = decay(diag)
    step = lam
    for _ in range(int(math.log2(planes))):
        step = step * step
    squares = [step]
    while 2 ** len(squares) <= count:
        squares.append(squares[-1] * squares[-1])

    def power(exponent, bits):
        result = jnp.ones_like(step)
        for bit in range(bits):
            result = result * jnp.where((exponent >> bit) & 1 == 1, squares[bit], 1.0)
        return result

    left = jnp.zeros_like(step)
    right = jnp.zeros_like(step)
    ahead, back = ends[0], ends[1]
    bits = int(math.log2(count))
    for bit in range(bits):
        size = 1 << bit
        other = xor_permute(jnp.stack([ahead, back]), "span", size)
        is_right = (me >> bit) & 1 == 1
        place = me & (size - 1)
        reach = power(jnp.where(is_right, place, size - 1 - place), bit)
        left = jnp.where(is_right, left + reach * other[0], left)
        right = jnp.where(is_right, right, right + reach * other[1])
        ahead, back = (
            jnp.where(is_right, ahead + squares[bit] * other[0], other[0] + squares[bit] * ahead),
            jnp.where(is_right, other[1] + squares[bit] * back, back + squares[bit] * other[1]),
        )
    wrap = 1.0 / (1.0 - squares[bits])
    left = left + power(me, bits) * ahead * wrap
    right = right + power(count - 1 - me, bits) * back * wrap
    return left, right


def on_device(
    scalar, span_vel, flux_weight, neighbours, diagonal, interface, schur_one, schur_two, schur_three, schur_root
):
    planes, cells = scalar.shape
    count, me = lax.axis_size("span"), lax.axis_index("span")
    dom = lax.axis_index("dom")
    waves = schur_one.shape[0]
    rows, wave_rows = -(-planes // SUB) * SUB, -(-waves // SUB) * SUB
    nblocks = cells // LANES
    domains, slots = interface.shape
    pair_cells = domains // 2 * slots
    pad = lambda value: value if rows == planes else jnp.pad(value, ((0, rows - planes), (0, 0)))
    field, sv = pad(scalar), pad(span_vel)
    diag = diagonal.reshape(nblocks, LANES)
    offsets = xor_offsets(count)

    def boundary(value):
        edge = jnp.where(dom == 0, value[:, cells - LANES :], value[:, :LANES])
        return xor_permute(edge, "dom", 1)

    block_rows = 2 * rows + 3 * SUB
    payload, local, edge, dif = call(
        functools.partial(source_kernel, planes),
        [
            ((block_rows, 2 * LANES), F32),
            ((rows, cells), F32),
            ((6, nblocks, LANES), F32),
            ((domains, LANES), F32),
        ],
        (field, boundary(field), sv, flux_weight, neighbours, diag, interface),
        [pltpu.VMEM((rows + 2 * SUB, cells + 2 * LANES), F32), pltpu.VMEM((SUB, cells), F32)],
        name="source",
    )
    mine, received = gathered(payload, "span")

    (slot_of,) = call(slot_kernel, [((nblocks, LANES), jnp.int32)], (interface,), name="slots")
    own_wave = me * waves + jnp.arange(waves, dtype=jnp.int32)
    xored = me ^ jnp.array(offsets, jnp.int32)
    plane_of = xored[:, None] * planes + jnp.arange(rows, dtype=jnp.int32)[None, :]
    valid = jnp.arange(rows) < planes
    table = jnp.where(valid[None, None], fourier_entry(own_wave[:, None, None], plane_of[None]), 0.0)
    table = jnp.pad(table.reshape(waves, count * rows), ((0, wave_rows - waves), (0, 0)))
    edge_planes = (jnp.arange(count)[:, None] * planes + jnp.array([0, planes - 1])[None, :]).reshape(-1)
    edge_table = fourier_entry(own_wave[:, None], edge_planes[None, :].astype(jnp.int32))
    sigma = wave_shift(own_wave)
    smem = pl.BlockSpec(memory_space=pltpu.SMEM)
    hbm = pl.BlockSpec(memory_space=pl.ANY)
    vmem = pl.BlockSpec(memory_space=pltpu.VMEM)
    chunks = 4
    tree = [pltpu.VMEM(value.shape, F32) for value in (schur_one, schur_two, schur_three, schur_root)]
    s3, keep = call(
        functools.partial(up_kernel, offsets, rows),
        [((wave_rows, LANES), F32), ((waves, SUB, LANES), F32)],
        (me.reshape(1), mine, received, table, edge_table, sigma, dif, schur_one, schur_two, schur_three),
        tree[:3]
        + [
            pltpu.SemaphoreType.DMA((3, chunks)),
            pltpu.VMEM((count * rows, pair_cells), F32),
            pltpu.VMEM((count, 3 * SUB, 2 * LANES), F32),
            pltpu.VMEM((waves, SUB, LANES), F32),
            pltpu.VMEM((pair_cells // LANES, wave_rows, LANES), F32),
        ],
        [smem, vmem, vmem, vmem, smem, smem, vmem, hbm, hbm, hbm],
        name="up",
    )
    other = xor_permute(s3, "dom", 1)
    (returned,) = call(
        down_kernel,
        [((pair_cells // LANES, wave_rows, LANES), F32)],
        (s3, other, keep, schur_root, schur_three, schur_two, schur_one),
        tree[::-1] + [pltpu.SemaphoreType.DMA((4, chunks))],
        [vmem, vmem, vmem, hbm, hbm, hbm, hbm],
        name="down",
    )
    mine, received = gathered(returned.reshape(-1, LANES), "span")

    up_ring = [(i, (i + 1) % count) for i in range(count)]
    down_ring = [(j, i) for i, j in up_ring]
    q_first, q_last, v_first, v_last, sv_first, sv_last = (edge[i] for i in range(6))
    lam, kappa = decay(diag)
    at_first = kappa * 0.5 * sv_first * lax.ppermute(v_last, "span", up_ring)
    at_last = -kappa * 0.5 * sv_last * lax.ppermute(v_first, "span", down_ring)
    reach = jnp.ones_like(lam)
    for bit in range(int(math.log2(planes))):
        factor = lam
        for _ in range(bit):
            factor = factor * factor
        reach = reach * factor
    ends = jnp.stack([q_last + reach * at_first + at_last, q_first + at_first + reach * at_last])
    left, right = inflow(ends, diag, planes)
    flows = jnp.stack([left, right, at_first, at_last])

    wave_of = xored[:, None] * waves + jnp.arange(wave_rows, dtype=jnp.int32)[None, :]
    row_ids = jnp.arange(rows + SUB, dtype=jnp.int32)
    row_plane = jnp.where(row_ids < rows, row_ids, jnp.where(row_ids == rows, -1, planes))
    row_plane = (me * planes + row_plane + PLANES) % PLANES
    back_table = fourier_entry(wave_of[None], row_plane[:, None, None])
    back_table = jnp.where((jnp.arange(wave_rows) < waves)[None, None], back_table, 0.0)
    back_table = back_table.reshape(rows + SUB, count * wave_rows)
    pressure, outer = call(
        functools.partial(pressure_kernel, planes, domains, count),
        [((rows, cells), F32), ((SUB, cells), F32)],
        (mine, received, back_table, local, flows, diag, slot_of),
        [pltpu.VMEM((rows + SUB, pair_cells), F32), pltpu.VMEM((count * wave_rows, pair_cells), F32)],
        name="pressure",
    )
    (corrected,) = call(
        functools.partial(corrected_kernel, planes),
        [((rows, cells), F32)],
        (field, pressure, outer, boundary(pressure), sv, flux_weight, neighbours),
        [pltpu.VMEM((rows + 2 * SUB, cells + 2 * LANES), F32)],
        name="corrected",
    )
    return (pressure[:planes], corrected[:planes])


def solution(mesh):
    placed = (
        P(("case", "span"), "dom"),
        P(("case", "span"), "dom"),
        P(None, "dom"),
        P(None, "dom"),
        P("dom"),
        P("dom", None),
        P("span", "dom", None, None),
        P("span", "dom", None, None),
        P("span", "dom", None, None),
        P("span", None, None, None),
    )
    return jax.shard_map(
        on_device,
        mesh=mesh,
        in_specs=placed,
        out_specs=(P(("case", "span"), "dom"), P(("case", "span"), "dom")),
        check_vma=False,
    )
```

```python
import functools
import math

import jax
import jax.numpy as jnp
from jax import lax
from jax.experimental import pallas as pl
from jax.experimental.pallas import tpu as pltpu
from jax.sharding import PartitionSpec as P


PLANES = 128
LANES = 128
SUB = 8
HALF = LANES // 2
F32 = jnp.float32
EXACT = lax.Precision.HIGHEST


def fourier_entry(wave_ids, plane_ids):
    middle = PLANES // 2
    wave_num = jnp.where(wave_ids <= middle, wave_ids, wave_ids - middle)
    phase_angle = (wave_num * plane_ids % PLANES).astype(F32) * (2.0 * math.pi / PLANES)
    at_edge = (wave_ids == 0) | (wave_ids == middle)
    weight_row = jnp.where(at_edge, math.sqrt(1.0 / PLANES), math.sqrt(2.0 / PLANES))
    return jnp.where(wave_ids <= middle, jnp.cos(phase_angle), jnp.sin(phase_angle)) * weight_row


def wave_shift(wave_ids):
    middle = PLANES // 2
    wave_num = jnp.where(wave_ids <= middle, wave_ids, wave_ids - middle).astype(F32)
    return (2.0 * jnp.sin(wave_num * (math.pi / PLANES))) ** 2


def xor_permute(value, axis, mask):
    return lax.ppermute(value, axis, [(i, i ^ mask) for i in range(lax.axis_size(axis))])


def gathered(block, axis):
    count = lax.axis_size(axis)
    far = [xor_permute(block, axis, mask) for mask in range(count - 2, 0, -2)]
    mine = jnp.concatenate([block] + far[::-1], axis=0)
    return mine, xor_permute(mine, axis, 1)


def xor_offsets(count):
    return list(range(0, count, 2)) + list(range(1, count, 2))


def whole(*shapes):
    return [pl.BlockSpec(memory_space=pltpu.VMEM) for _ in shapes]


def lane_take(source, index):
    return jnp.take_along_axis(source, index, axis=1, mode="promise_in_bounds")


def decay(diag):
    root = jnp.sqrt(diag + 0.25 * diag * diag)
    return 1.0 / (1.0 + 0.5 * diag + root), 0.5 / root


def powers(base, exponent, limit):
    result = None
    bit, factor = 1, base
    while bit < limit:
        part = jnp.where((exponent & bit) != 0, factor, 1.0)
        result = part if result is None else result * part
        factor = factor * factor
        bit *= 2
    return result


def convection(ext, block, nblocks, rows, sv, fw_ref, nb_ref):
    start = pl.multiple_of(block * LANES, LANES)
    here = pl.multiple_of(start + LANES, LANES)
    field = ext[pl.ds(SUB, rows), pl.ds(here, LANES)]
    before = ext[pl.ds(SUB, rows), pl.ds(start, LANES)]
    after = ext[pl.ds(SUB, rows), pl.ds(pl.multiple_of(here + LANES, LANES), LANES)]
    lane = lax.broadcasted_iota(jnp.int32, (rows, LANES), 1)
    around = jnp.where(lane < HALF, after, before)
    ahead = ext[pl.ds(SUB + 1, rows), pl.ds(here, LANES)]
    behind = ext[pl.ds(SUB - 1, rows), pl.ds(here, LANES)]
    total = sv * 0.5 * (ahead - behind)
    for slot in range(fw_ref.shape[0]):
        ids = nb_ref[pl.ds(slot, 1), pl.ds(start, LANES)]
        index = jnp.broadcast_to(ids & (LANES - 1), (rows, LANES))
        inside = (((ids >> 7) - block) & (nblocks - 1)) == 0
        near = jnp.where(inside, lane_take(field, index), lane_take(around, index))
        total = total + fw_ref[pl.ds(slot, 1), pl.ds(start, LANES)] * (near - field)
    return field, total


def fill(ext, field_ref, halo_ref, rows, cells):
    ext[pl.ds(SUB, rows), pl.ds(LANES, cells)] = field_ref[...]
    ext[pl.ds(SUB, rows), pl.ds(0, LANES)] = halo_ref[...]
    ext[pl.ds(SUB, rows), pl.ds(LANES + cells, LANES)] = halo_ref[...]


def source_kernel(
    planes, halo_ref, v_hbm, sv_hbm, fw_hbm, nb_hbm, diag_hbm, iface_hbm,
    pay_ref, q_ref, edge_ref, dif_ref, v_ref, sv_ref, fw_ref, nb_ref, diag_ref, iface_ref, ext, strip, sems,
):
    rows, cells = v_ref.shape
    moved = (
        (v_hbm, v_ref), (sv_hbm, sv_ref), (fw_hbm, fw_ref), (nb_hbm, nb_ref), (diag_hbm, diag_ref), (iface_hbm, iface_ref),
    )
    moves = [pltpu.make_async_copy(src, dst, sems.at[i]) for i, (src, dst) in enumerate(moved)]
    for move in moves:
        move.start()
    for move in moves:
        move.wait()
    nblocks = cells // LANES
    fill(ext, v_ref, halo_ref, rows, cells)
    ext[pl.ds(0, SUB), :] = jnp.zeros((SUB, cells + 2 * LANES), F32)
    ext[pl.ds(SUB + rows, SUB), :] = jnp.zeros((SUB, cells + 2 * LANES), F32)
    row = lax.broadcasted_iota(jnp.int32, (rows, LANES), 0)

    def step(block, carry):
        start = pl.multiple_of(block * LANES, LANES)
        sv = sv_ref[:, pl.ds(start, LANES)]
        field, total = convection(ext, block, nblocks, rows, sv, fw_ref, nb_ref)
        source = field - total
        diag = diag_ref[pl.ds(block, 1), :]
        lam, kappa = decay(diag)
        forward, backward, factor, shift = source, source, lam, 1
        while shift < planes:
            down = jnp.where(row >= shift, pltpu.roll(forward, shift, 0), 0.0)
            up = jnp.where(row < rows - shift, pltpu.roll(backward, rows - shift, 0), 0.0)
            forward = forward + factor * down
            backward = backward + factor * up
            factor, shift = factor * factor, shift * 2
        local = kappa * (forward + (backward - source))
        q_ref[:, pl.ds(start, LANES)] = local
        last = planes - 1
        edges = (
            local[0:1], local[last:planes], field[0:1], field[last:planes], sv[0:1], sv[last:planes], diag,
        )
        for place, value in enumerate(edges):
            strip[pl.ds(place, 1), pl.ds(start, LANES)] = value
            if place < 6:
                edge_ref[place, pl.ds(block, 1), :] = value
        return carry

    lax.fori_loop(0, nblocks, step, 0, unroll=4)
    domains = iface_ref.shape[0]
    width = cells // domains
    for pair in range(domains // 2):
        total = None
        for domain in (2 * pair, 2 * pair + 1):
            where = iface_ref[pl.ds(domain, 1), :] & (width - 1)
            lane, which = where & (LANES - 1), where >> 7
            inner = jnp.zeros((rows, LANES), F32)
            outer = jnp.zeros((SUB, LANES), F32)
            for part in range(width // LANES):
                start = domain * width + part * LANES
                here = which == part
                index = jnp.broadcast_to(lane, (rows, LANES))
                inner = jnp.where(here, lane_take(q_ref[:, pl.ds(start, LANES)], index), inner)
                index = jnp.broadcast_to(lane, (SUB, LANES))
                outer = jnp.where(here, lane_take(strip[:, pl.ds(start, LANES)], index), outer)
            total = inner if total is None else total + inner
            for place in range(6):
                at = 2 * rows + SUB * (place // 2) + domain
                pay_ref[pl.ds(at, 1), pl.ds((place % 2) * LANES, LANES)] = outer[place : place + 1]
            dif_ref[pl.ds(domain, 1), :] = outer[6:7]
        half, column = divmod(pair, domains // 4)
        pay_ref[pl.ds(half * rows, rows), pl.ds(column * LANES, LANES)] = total


def slots_of(iface_ref, inv_ref):
    domains, slots = iface_ref.shape
    per = inv_ref.shape[0] // domains
    columns = jnp.transpose(jnp.concatenate([iface_ref[...].astype(F32)] * (LANES // domains), axis=0))
    lane = lax.broadcasted_iota(jnp.int32, (slots, LANES), 1)
    slot = lax.broadcasted_iota(jnp.int32, (slots, LANES), 0).astype(F32)
    for domain in range(domains):
        own = columns[:, domain : domain + 1].astype(jnp.int32) & (per * LANES - 1)
        own = jnp.broadcast_to(own, (slots, LANES))
        for part in range(per):
            hit = jnp.where(own == lane + part * LANES, slot, -1.0)
            found = jnp.max(hit, axis=0, keepdims=True)
            inv_ref[pl.ds(domain * per + part, 1), :] = found.astype(jnp.int32)


def stage_kernel(
    iface_ref, m1_hbm, m2_hbm, m3_hbm, root_hbm, inv_ref, m1, flipped, m3, root, m2, sems
):
    moved = ((m2_hbm, m2), (m1_hbm, m1), (m3_hbm, m3), (root_hbm, root))
    moves = [pltpu.make_async_copy(src, dst, sems.at[i]) for i, (src, dst) in enumerate(moved)]
    for move in moves:
        move.start()
    slots_of(iface_ref, inv_ref)
    moves[0].wait()

    def flip(wave, carry):
        for node in range(m2.shape[1]):
            flipped[wave, node] = jnp.transpose(m2[wave, node])
        return carry

    lax.fori_loop(0, m2.shape[0], flip, 0, unroll=2)
    for move in moves[1:]:
        move.wait()


def over_lanes(matrix, row):
    return jnp.sum(matrix * row, axis=1, keepdims=True)


def over_rows(matrix, column):
    return jnp.sum(matrix * column, axis=0, keepdims=True)


def up_kernel(
    offsets, rows, me_ref, mine_ref, recv_ref, table_ref, edge_ref, sigma_ref, dif_ref, m1, flipped, m3,
    s3_ref, keep_ref, q, edges, pairs, spectrum, columns,
):
    waves, nodes = m1.shape[:2]
    count = len(offsets)
    me = me_ref[0]
    block_rows = 2 * rows + 3 * SUB
    for place, offset in enumerate(offsets):
        source = mine_ref if place < count // 2 else recv_ref
        base = (place % (count // 2)) * block_rows
        for half in range(2):
            q[pl.ds(place * rows, rows), pl.ds(half * 2 * LANES, 2 * LANES)] = source[
                pl.ds(base + half * rows, rows), :
            ]
        edges[me ^ offset] = source[pl.ds(base + 2 * rows, 3 * SUB), :]
    wide = jnp.dot(table_ref[...], q[...], precision=EXACT, preferred_element_type=F32)
    for node in range(nodes):
        spectrum[node] = wide[:, node * LANES : (node + 1) * LANES]
    dif = dif_ref[...]
    lam, _ = decay(dif)
    first_of = lambda t, place: edges[t, pl.ds(SUB * place, SUB), pl.ds(0, LANES)]
    last_of = lambda t, place: edges[t, pl.ds(SUB * place, SUB), pl.ds(LANES, LANES)]
    residual = []
    for t in range(count):
        prev, succ = (t - 1) % count, (t + 1) % count
        residual.append(last_of(prev, 0) - lam * first_of(t, 0) + 0.5 * first_of(t, 2) * last_of(prev, 1))
        residual.append(first_of(succ, 0) - lam * last_of(t, 0) - 0.5 * last_of(t, 2) * first_of(succ, 1))

    def edge_step(wave, carry):
        total = edge_ref[wave, 0] * residual[0]
        for place in range(1, 2 * count):
            total = total + edge_ref[wave, place] * residual[place]
        leaf = total / (dif + sigma_ref[wave])
        pairs[wave] = leaf + pltpu.roll(leaf, SUB - 1, 0)
        return carry

    lax.fori_loop(0, waves, edge_step, 0, unroll=2)
    columns[...] = jnp.zeros((LANES, LANES), F32)
    lane = lax.broadcasted_iota(jnp.int32, (LANES, LANES), 1)

    def wave_step(wave, carry):
        sums = []
        for node in range(nodes):
            leaf = spectrum[node, pl.ds(wave, 1), :] + pairs[wave, pl.ds(2 * node, 1), :]
            matrix = m1[wave, node]
            first = over_lanes(matrix, leaf)
            keep_ref[wave, pl.ds(node, 1), :] = over_rows(matrix, first)
            sums.append(first)
        total = None
        for node in range(nodes // 2):
            second = over_rows(flipped[wave, node], sums[2 * node] + sums[2 * node + 1])
            keep_ref[wave, pl.ds(nodes + node, 1), :] = second
            total = second if total is None else total + second
        third = over_lanes(m3[wave, 0], total)
        columns[...] = jnp.where(lane == wave, third, columns[...])
        return carry

    lax.fori_loop(0, waves, wave_step, 0, unroll=2)
    s3_ref[...] = jnp.transpose(columns[...])[: s3_ref.shape[0]]


def down_kernel(s3_ref, other_ref, keep_ref, m1, flipped, m3, root, out_ref, lowered):
    waves, nodes = m1.shape[:2]
    lowered[...] = jnp.zeros((LANES, LANES), F32)
    if out_ref.shape[1] > waves:
        out_ref[...] = jnp.zeros(out_ref.shape, F32)

    def root_step(wave, carry):
        own = s3_ref[pl.ds(wave, 1), :]
        top = over_lanes(root[wave, 0], own + other_ref[pl.ds(wave, 1), :])
        lowered[pl.ds(wave, 1), :] = own - over_rows(root[wave, 0], top)
        return carry

    lax.fori_loop(0, waves, root_step, 0, unroll=4)
    lowered[...] = jnp.transpose(lowered[...])
    lane = lax.broadcasted_iota(jnp.int32, (LANES, LANES), 1)

    def wave_step(wave, carry):
        third = jnp.sum(jnp.where(lane == wave, lowered[...], 0.0), axis=1, keepdims=True)
        third = over_rows(m3[wave, 0], third)
        for pair in range(nodes // 2):
            second = over_lanes(flipped[wave, pair], keep_ref[wave, pl.ds(nodes + pair, 1), :] - third)
            for node in (2 * pair, 2 * pair + 1):
                first = keep_ref[wave, pl.ds(node, 1), :] - over_rows(m1[wave, node], second)
                out_ref[node, pl.ds(wave, 1), :] = first
        return carry

    lax.fori_loop(0, waves, wave_step, 0, unroll=2)


def change_of(pairs, count, mine_ref, recv_ref, table_ref, waves):
    nodes = mine_ref.shape[0] * 2 // waves.shape[0]
    wave_rows = waves.shape[0] // count
    for place in range(count):
        source = mine_ref if place < count // 2 else recv_ref
        base = (place % (count // 2)) * nodes * wave_rows
        for at, pair in enumerate(pairs):
            waves[pl.ds(place * wave_rows, wave_rows), pl.ds(at * LANES, LANES)] = source[
                pl.ds(base + pair * wave_rows, wave_rows), :
            ]
    return jnp.dot(table_ref[...], waves[...], precision=EXACT, preferred_element_type=F32)


def pressure_block(planes, block, change, q_ref, inflow_ref, diag_ref, inv_ref):
    rows = q_ref.shape[0]
    start = block * LANES if isinstance(block, int) else pl.multiple_of(block * LANES, LANES)
    row = lax.broadcasted_iota(jnp.int32, (rows, LANES), 0)
    edge_row = lax.broadcasted_iota(jnp.int32, (SUB, LANES), 0)
    lam, _ = decay(diag_ref[pl.ds(block, 1), :])
    left, right, at_first, at_last = (inflow_ref[i, pl.ds(block, 1), :] for i in range(4))
    from_left = at_first + lam * left
    from_right = at_last + lam * right
    local = q_ref[:, pl.ds(start, LANES)]
    value = local + powers(lam, row, planes) * from_left + powers(lam, (planes - 1) - row, planes) * from_right
    span = lam
    for _ in range(int(math.log2(planes))):
        span = span * span
    before = lam * local[0:1] + left + lam * at_first + span * from_right
    after = lam * local[planes - 1 : planes] + right + lam * at_last + span * from_left
    outer = jnp.where(edge_row == 0, before, after)
    slot = inv_ref[pl.ds(block, 1), :]
    taken = slot >= 0
    got = lane_take(change, jnp.broadcast_to(jnp.maximum(slot, 0), change.shape))
    value = jnp.where(taken, 0.5 * value + 0.5 * got[:rows], value)
    return value, jnp.where(taken, 0.5 * outer + 0.5 * got[rows:], outer)


def rim_kernel(
    planes, domains, count, dom_ref, mine_ref, recv_ref, table_ref, q_ref, inflow_ref, diag_ref, inv_ref,
    rim_ref, waves,
):
    nblocks = q_ref.shape[1] // LANES
    for side, block, pair in ((0, nblocks - 1, domains // 2 - 1), (1, 0, 0)):

        @pl.when(dom_ref[0] == side)
        def _(block=block, pair=pair):
            change = change_of((pair,), count, mine_ref, recv_ref, table_ref, waves)
            rim_ref[...] = pressure_block(planes, block, change, q_ref, inflow_ref, diag_ref, inv_ref)[0]


def pressure_kernel(
    planes, domains, count, mine_ref, recv_ref, table_ref, q_ref, inflow_ref, diag_ref, inv_ref,
    ext, change, waves,
):
    rows, cells = q_ref.shape
    nblocks = cells // LANES
    per_pair = 2 * nblocks // domains
    change[...] = change_of(range(domains // 2), count, mine_ref, recv_ref, table_ref, waves)

    def step(block, carry):
        column = pl.multiple_of((block // per_pair) * LANES, LANES)
        value, outer = pressure_block(
            planes, block, change[:, pl.ds(column, LANES)], q_ref, inflow_ref, diag_ref, inv_ref
        )
        here = pl.multiple_of((block + 1) * LANES, LANES)
        ext[pl.ds(SUB, rows), pl.ds(here, LANES)] = value
        ext[pl.ds(SUB - 1, 1), pl.ds(here, LANES)] = outer[0:1]
        ext[pl.ds(SUB + planes, 1), pl.ds(here, LANES)] = outer[1:2]
        return carry

    lax.fori_loop(0, nblocks, step, 0, unroll=4)


def corrected_kernel(ext_in, v_ref, halo_ref, sv_ref, fw_ref, nb_ref, p_hbm, out_ref, ext, sems):
    rows, cells = v_ref.shape
    nblocks = cells // LANES
    store = pltpu.make_async_copy(ext_in.at[pl.ds(SUB, rows), pl.ds(LANES, cells)], p_hbm, sems.at[0])
    store.start()
    ext[:, pl.ds(LANES, cells)] = ext_in[:, pl.ds(LANES, cells)]
    ext[pl.ds(SUB, rows), pl.ds(0, LANES)] = halo_ref[...]
    ext[pl.ds(SUB, rows), pl.ds(LANES + cells, LANES)] = halo_ref[...]

    def step(block, carry):
        start = pl.multiple_of(block * LANES, LANES)
        sv = sv_ref[:, pl.ds(start, LANES)]
        _, total = convection(ext, block, nblocks, rows, sv, fw_ref, nb_ref)
        out_ref[:, pl.ds(start, LANES)] = v_ref[:, pl.ds(start, LANES)] - total
        return carry

    lax.fori_loop(0, nblocks, step, 0, unroll=4)
    store.wait()


HBM = pl.BlockSpec(memory_space=pltpu.HBM)


def in_hbm(value):
    return pltpu.with_memory_space_constraint(value, pltpu.HBM)


PARAMS = pltpu.CompilerParams(vmem_limit_bytes=40 * 1024 * 1024)


def call(kernel, outs, args, scratch=(), specs=None, out_specs=None):
    return pl.pallas_call(
        kernel,
        out_shape=[jax.ShapeDtypeStruct(*out) for out in outs],
        in_specs=specs or whole(*args),
        out_specs=out_specs or whole(*outs),
        scratch_shapes=list(scratch),
        compiler_params=PARAMS,
    )(*(in_hbm(arg) if spec is HBM else arg for arg, spec in zip(args, specs or whole(*args))))


def inflow(ends, diag, planes):
    count, me = lax.axis_size("span"), lax.axis_index("span")
    lam, _ = decay(diag)
    step = lam
    for _ in range(int(math.log2(planes))):
        step = step * step
    squares = [step]
    while 2 ** len(squares) <= count:
        squares.append(squares[-1] * squares[-1])

    def power(exponent, bits):
        result = jnp.ones_like(step)
        for bit in range(bits):
            result = result * jnp.where((exponent >> bit) & 1 == 1, squares[bit], 1.0)
        return result

    left = jnp.zeros_like(step)
    right = jnp.zeros_like(step)
    ahead, back = ends[0], ends[1]
    bits = int(math.log2(count))
    for bit in range(bits):
        size = 1 << bit
        other = xor_permute(jnp.stack([ahead, back]), "span", size)
        is_right = (me >> bit) & 1 == 1
        place = me & (size - 1)
        reach = power(jnp.where(is_right, place, size - 1 - place), bit)
        left = jnp.where(is_right, left + reach * other[0], left)
        right = jnp.where(is_right, right, right + reach * other[1])
        ahead, back = (
            jnp.where(is_right, ahead + squares[bit] * other[0], other[0] + squares[bit] * ahead),
            jnp.where(is_right, other[1] + squares[bit] * back, back + squares[bit] * other[1]),
        )
    wrap = 1.0 / (1.0 - squares[bits])
    left = left + power(me, bits) * ahead * wrap
    right = right + power(count - 1 - me, bits) * back * wrap
    return left, right


def on_device(
    scalar, span_vel, flux_weight, neighbours, diagonal, interface, schur_one, schur_two, schur_three, schur_root
):
    planes, cells = scalar.shape
    count, me = lax.axis_size("span"), lax.axis_index("span")
    dom = lax.axis_index("dom")
    waves = schur_one.shape[0]
    rows, wave_rows = -(-planes // SUB) * SUB, -(-waves // SUB) * SUB
    nblocks = cells // LANES
    domains, slots = interface.shape
    pair_cells = domains // 2 * slots
    pad = lambda value: value if rows == planes else jnp.pad(value, ((0, rows - planes), (0, 0)))
    field, sv = pad(scalar), pad(span_vel)
    diag = diagonal.reshape(nblocks, LANES)
    offsets = xor_offsets(count)

    def boundary(value):
        edge = jnp.where(dom == 0, value[:, cells - LANES :], value[:, :LANES])
        return xor_permute(edge, "dom", 1)

    block_rows = 2 * rows + 3 * SUB
    vmem = pl.BlockSpec(memory_space=pltpu.VMEM)
    smem = pl.BlockSpec(memory_space=pltpu.SMEM)
    payload, local, edge, dif, field_in, sv_in, fw_in, nb_in, diag_in, iface_in = call(
        functools.partial(source_kernel, planes),
        [
            ((block_rows, 2 * LANES), F32),
            ((rows, cells), F32),
            ((6, nblocks, LANES), F32),
            ((domains, LANES), F32),
            ((rows, cells), F32),
            ((rows, cells), F32),
            (flux_weight.shape, F32),
            (neighbours.shape, jnp.int32),
            ((nblocks, LANES), F32),
            (interface.shape, jnp.int32),
        ],
        (boundary(field), field, sv, flux_weight, neighbours, diag, interface),
        [
            pltpu.VMEM((rows + 2 * SUB, cells + 2 * LANES), F32),
            pltpu.VMEM((SUB, cells), F32),
            pltpu.SemaphoreType.DMA((6,)),
        ],
        [vmem] + [HBM] * 6,
    )
    mine, received = gathered(payload, "span")

    slot_of, m1, flipped, m3, root = call(
        stage_kernel,
        [
            ((nblocks, LANES), jnp.int32),
            (schur_one.shape, F32),
            (schur_two.shape, F32),
            (schur_three.shape, F32),
            (schur_root.shape, F32),
        ],
        (iface_in, schur_one, schur_two, schur_three, schur_root),
        [pltpu.VMEM(schur_two.shape, F32), pltpu.SemaphoreType.DMA((4,))],
        [vmem] + [HBM] * 4,
    )
    own_wave = me * waves + jnp.arange(waves, dtype=jnp.int32)
    xored = me ^ jnp.array(offsets, jnp.int32)
    plane_of = xored[:, None] * planes + jnp.arange(rows, dtype=jnp.int32)[None, :]
    valid = jnp.arange(rows) < planes
    table = jnp.where(valid[None, None], fourier_entry(own_wave[:, None, None], plane_of[None]), 0.0)
    table = jnp.pad(table.reshape(waves, count * rows), ((0, wave_rows - waves), (0, 0)))
    edge_planes = (jnp.arange(count)[:, None] * planes + jnp.array([0, planes - 1])[None, :]).reshape(-1)
    edge_table = fourier_entry(own_wave[:, None], edge_planes[None, :].astype(jnp.int32))
    sigma = wave_shift(own_wave)
    s3, keep = call(
        functools.partial(up_kernel, offsets, rows),
        [((wave_rows, LANES), F32), ((waves, SUB, LANES), F32)],
        (me.reshape(1), mine, received, table, edge_table, sigma, dif, m1, flipped, m3),
        [
            pltpu.VMEM((count * rows, pair_cells), F32),
            pltpu.VMEM((count, 3 * SUB, 2 * LANES), F32),
            pltpu.VMEM((waves, SUB, LANES), F32),
            pltpu.VMEM((pair_cells // LANES, wave_rows, LANES), F32),
            pltpu.VMEM((LANES, LANES), F32),
        ],
        [smem, vmem, vmem, vmem, smem, smem] + [vmem] * 4,
    )
    other = xor_permute(s3, "dom", 1)
    (returned,) = call(
        down_kernel,
        [((pair_cells // LANES, wave_rows, LANES), F32)],
        (s3, other, keep, m1, flipped, m3, root),
        [pltpu.VMEM((LANES, LANES), F32)],
    )
    mine, received = gathered(returned.reshape(-1, LANES), "span")

    up_ring = [(i, (i + 1) % count) for i in range(count)]
    down_ring = [(j, i) for i, j in up_ring]
    q_first, q_last, v_first, v_last, sv_first, sv_last = (edge[i] for i in range(6))
    lam, kappa = decay(diag_in)
    v_before, v_after = lax.ppermute(v_last, "span", up_ring), lax.ppermute(v_first, "span", down_ring)
    at_first = kappa * 0.5 * sv_first * v_before
    at_last = -kappa * 0.5 * sv_last * v_after
    reach = jnp.ones_like(lam)
    for bit in range(int(math.log2(planes))):
        factor = lam
        for _ in range(bit):
            factor = factor * factor
        reach = reach * factor
    ends = jnp.stack([q_last + reach * at_first + at_last, q_first + at_first + reach * at_last])
    left, right = inflow(ends, diag_in, planes)
    flows = jnp.stack([left, right, at_first, at_last])

    wave_of = xored[:, None] * waves + jnp.arange(wave_rows, dtype=jnp.int32)[None, :]
    row_ids = jnp.arange(rows + SUB, dtype=jnp.int32)
    row_plane = jnp.where(row_ids < rows, row_ids, jnp.where(row_ids == rows, -1, planes))
    row_plane = (me * planes + row_plane + PLANES) % PLANES
    back_table = fourier_entry(wave_of[None], row_plane[:, None, None])
    back_table = jnp.where((jnp.arange(wave_rows) < waves)[None, None], back_table, 0.0)
    back_table = back_table.reshape(rows + SUB, count * wave_rows)
    wave_scratch = lambda pairs: pltpu.VMEM((count * wave_rows, pairs * LANES), F32)
    parts = (mine, received, back_table, local, flows, diag_in, slot_of)
    (rim,) = call(
        functools.partial(rim_kernel, planes, domains, count),
        [((rows, LANES), F32)],
        (dom.reshape(1),) + parts,
        [wave_scratch(1)],
        [smem] + [vmem] * 7,
    )
    halo = xor_permute(rim, "dom", 1)
    ext_shape = (rows + 2 * SUB, cells + 2 * LANES)
    (extended,) = call(
        functools.partial(pressure_kernel, planes, domains, count),
        [(ext_shape, F32)],
        parts,
        [pltpu.VMEM((rows + SUB, pair_cells), F32), wave_scratch(domains // 2)],
    )
    pressure, corrected = call(
        corrected_kernel,
        [((rows, cells), F32), ((rows, cells), F32)],
        (extended, field_in, halo, sv_in, fw_in, nb_in),
        [pltpu.VMEM(ext_shape, F32), pltpu.SemaphoreType.DMA((1,))],
        out_specs=[HBM, vmem],
    )
    return (pressure[:planes], corrected[:planes])


def solution(mesh):
    placed = (
        P(("case", "span"), "dom"),
        P(("case", "span"), "dom"),
        P(None, "dom"),
        P(None, "dom"),
        P("dom"),
        P("dom", None),
        P("span", "dom", None, None),
        P("span", "dom", None, None),
        P("span", "dom", None, None),
        P("span", None, None, None),
    )

    return jax.shard_map(
        on_device,
        mesh=mesh,
        in_specs=placed,
        out_specs=(P(("case", "span"), "dom"), P(("case", "span"), "dom")),
        check_vma=False,
    )
```

```python
import functools
import math

import jax
import jax.numpy as jnp
from jax import lax
from jax.experimental import pallas as pl
from jax.experimental.pallas import tpu as pltpu
from jax.sharding import PartitionSpec as P


PLANES = 128
LANES = 128
SUB = 8
HALF = LANES // 2
GROUP = 8
F32 = jnp.float32
BF16 = jnp.bfloat16
EXACT = lax.Precision.HIGHEST


def fourier_entry(wave_ids, plane_ids):
    middle = PLANES // 2
    wave_num = jnp.where(wave_ids <= middle, wave_ids, wave_ids - middle)
    phase_angle = (wave_num * plane_ids % PLANES).astype(F32) * (2.0 * math.pi / PLANES)
    at_edge = (wave_ids == 0) | (wave_ids == middle)
    weight_row = jnp.where(at_edge, math.sqrt(1.0 / PLANES), math.sqrt(2.0 / PLANES))
    return jnp.where(wave_ids <= middle, jnp.cos(phase_angle), jnp.sin(phase_angle)) * weight_row


def wave_shift(wave_ids):
    middle = PLANES // 2
    wave_num = jnp.where(wave_ids <= middle, wave_ids, wave_ids - middle).astype(F32)
    return (2.0 * jnp.sin(wave_num * (math.pi / PLANES))) ** 2


def xor_permute(value, axis, mask):
    return lax.ppermute(value, axis, [(i, i ^ mask) for i in range(lax.axis_size(axis))])


def gathered(block, axis):
    count = lax.axis_size(axis)
    far = [xor_permute(block, axis, mask) for mask in range(count - 2, 0, -2)]
    mine = jnp.concatenate([block] + far[::-1], axis=0)
    return mine, xor_permute(mine, axis, 1)


def xor_offsets(count):
    return list(range(0, count, 2)) + list(range(1, count, 2))


def whole(*shapes):
    return [pl.BlockSpec(memory_space=pltpu.VMEM) for _ in shapes]


def lane_take(source, index):
    return jnp.take_along_axis(source, index, axis=1, mode="promise_in_bounds")


def decay(diag):
    root = jnp.sqrt(diag + 0.25 * diag * diag)
    return 1.0 / (1.0 + 0.5 * diag + root), 0.5 / root


def powers(base, exponent, limit):
    result = None
    bit, factor = 1, base
    while bit < limit:
        part = jnp.where((exponent & bit) != 0, factor, 1.0)
        result = part if result is None else result * part
        factor = factor * factor
        bit *= 2
    return result


def column(block):
    return block * LANES if isinstance(block, int) else pl.multiple_of(block * LANES, LANES)


def convection(ext, at, block, nblocks, rows, sv, fw_ref, nb_ref):
    start, here = column(block), column(at)
    field = ext[pl.ds(SUB, rows), pl.ds(here, LANES)]
    before = ext[pl.ds(SUB, rows), pl.ds(column(at - 1), LANES)]
    after = ext[pl.ds(SUB, rows), pl.ds(column(at + 1), LANES)]
    lane = lax.broadcasted_iota(jnp.int32, (rows, LANES), 1)
    around = jnp.where(lane < HALF, after, before)
    ahead = ext[pl.ds(SUB + 1, rows), pl.ds(here, LANES)]
    behind = ext[pl.ds(SUB - 1, rows), pl.ds(here, LANES)]
    total = sv * 0.5 * (ahead - behind)
    for slot in range(fw_ref.shape[0]):
        ids = nb_ref[pl.ds(slot, 1), pl.ds(start, LANES)]
        index = jnp.broadcast_to(ids & (LANES - 1), (rows, LANES))
        inside = (((ids >> 7) - block) & (nblocks - 1)) == 0
        near = jnp.where(inside, lane_take(field, index), lane_take(around, index))
        total = total + fw_ref[pl.ds(slot, 1), pl.ds(start, LANES)] * (near - field)
    return field, total


def source_block(planes, ext, at, block, sv_ref, fw_ref, nb_ref, diag_ref, q_ref, edge_ref, strip):
    rows = q_ref.shape[0]
    nblocks = diag_ref.shape[0]
    row = lax.broadcasted_iota(jnp.int32, (rows, LANES), 0)
    start = column(block)
    sv = sv_ref[:, pl.ds(start, LANES)]
    field, total = convection(ext, at, block, nblocks, rows, sv, fw_ref, nb_ref)
    source = field - total
    diag = diag_ref[pl.ds(block, 1), :]
    lam, kappa = decay(diag)
    forward, backward, factor, shift = source, source, lam, 1
    while shift < planes:
        down = jnp.where(row >= shift, pltpu.roll(forward, shift, 0), 0.0)
        up = jnp.where(row < rows - shift, pltpu.roll(backward, rows - shift, 0), 0.0)
        forward = forward + factor * down
        backward = backward + factor * up
        factor, shift = factor * factor, shift * 2
    local = kappa * (forward + (backward - source))
    q_ref[:, pl.ds(start, LANES)] = local
    last = planes - 1
    edges = (
        local[0:1], local[last:planes], sv[0:1], sv[last:planes], field[0:1], field[last:planes], diag,
    )
    for place, value in enumerate(edges):
        strip[pl.ds(place, 1), pl.ds(start, LANES)] = value
        if place < edge_ref.shape[0]:
            edge_ref[place, pl.ds(block, 1), :] = value


def source_kernel(
    planes, v_hbm, sv_hbm, fw_hbm, nb_hbm, diag_hbm, iface_hbm,
    q_ref, edge_ref, strip, ext, v_ref, sv_ref, fw_ref, nb_ref, diag_ref, iface_ref, sems,
):
    rows, cells = v_ref.shape
    nblocks = cells // LANES
    moved = (
        (v_hbm, v_ref), (sv_hbm, sv_ref), (fw_hbm, fw_ref), (nb_hbm, nb_ref), (diag_hbm, diag_ref), (iface_hbm, iface_ref),
    )
    moves = [pltpu.make_async_copy(src, dst, sems.at[i]) for i, (src, dst) in enumerate(moved)]
    for move in moves:
        move.start()
    ext[pl.ds(0, SUB), :] = jnp.zeros((SUB, cells + 2 * LANES), F32)
    ext[pl.ds(SUB + rows, SUB), :] = jnp.zeros((SUB, cells + 2 * LANES), F32)
    for side in (0, LANES + cells):
        ext[pl.ds(SUB, rows), pl.ds(side, LANES)] = jnp.zeros((rows, LANES), F32)
    for move in moves:
        move.wait()
    ext[pl.ds(SUB, rows), pl.ds(LANES, cells)] = v_ref[...]

    def step(block, carry):
        source_block(
            planes, ext, block + 1, block, sv_ref, fw_ref, nb_ref, diag_ref, q_ref, edge_ref, strip
        )
        return carry

    lax.fori_loop(0, nblocks, step, 0, unroll=4)


def seam_kernel(
    planes, dom_ref, halo_ref, q_in, edge_in, strip_in, ext, sv_ref, fw_ref, nb_ref, diag_ref, iface_ref,
    q_ref, edge_ref, strip, pay_ref, dif_ref, window,
):
    rows, cells = q_ref.shape
    nblocks = cells // LANES
    for side, block in ((0, nblocks - 1), (1, 0)):

        @pl.when(dom_ref[0] == side)
        def _(side=side, block=block):
            near = side * LANES
            window[:, pl.ds(near, 2 * LANES)] = ext[:, pl.ds(column(block + side), 2 * LANES)]
            window[pl.ds(SUB, rows), pl.ds(2 * LANES * (1 - side), LANES)] = halo_ref[...]
            source_block(
                planes, window, 1, block, sv_ref, fw_ref, nb_ref, diag_ref, q_ref, edge_ref, strip
            )

    domains = iface_ref.shape[0]
    width = cells // domains
    for pair in range(domains // 2):
        total = None
        for domain in (2 * pair, 2 * pair + 1):
            where = iface_ref[pl.ds(domain, 1), :] & (width - 1)
            lane, which = where & (LANES - 1), where >> 7
            inner = jnp.zeros((rows, LANES), F32)
            outer = jnp.zeros((SUB, LANES), F32)
            for part in range(width // LANES):
                start = domain * width + part * LANES
                here = which == part
                index = jnp.broadcast_to(lane, (rows, LANES))
                inner = jnp.where(here, lane_take(q_ref[:, pl.ds(start, LANES)], index), inner)
                index = jnp.broadcast_to(lane, (SUB, LANES))
                outer = jnp.where(here, lane_take(strip[:, pl.ds(start, LANES)], index), outer)
            total = inner if total is None else total + inner
            for place in range(6):
                at = 2 * rows + SUB * (place // 2) + domain
                pay_ref[pl.ds(at, 1), pl.ds((place % 2) * LANES, LANES)] = outer[place : place + 1]
            dif_ref[pl.ds(domain, 1), :] = outer[6:7]
        half, side = divmod(pair, domains // 4)
        pay_ref[pl.ds(half * rows, rows), pl.ds(side * LANES, LANES)] = total


def slots_of(iface_ref, inv_ref):
    domains, slots = iface_ref.shape
    per = inv_ref.shape[0] // domains
    columns = jnp.transpose(jnp.concatenate([iface_ref[...].astype(F32)] * (LANES // domains), axis=0))
    lane = lax.broadcasted_iota(jnp.int32, (slots, LANES), 1)
    slot = lax.broadcasted_iota(jnp.int32, (slots, LANES), 0).astype(F32)
    for domain in range(domains):
        own = columns[:, domain : domain + 1].astype(jnp.int32) & (per * LANES - 1)
        own = jnp.broadcast_to(own, (slots, LANES))
        for part in range(per):
            hit = jnp.where(own == lane + part * LANES, slot, -1.0)
            found = jnp.max(hit, axis=0, keepdims=True)
            inv_ref[pl.ds(domain * per + part, 1), :] = found.astype(jnp.int32)


def split(value):
    high = value.astype(BF16)
    return high, (value - high.astype(F32)).astype(BF16)


def stage_kernel(
    iface_ref, m1_hbm, m2_hbm, m3_hbm, root_hbm, inv_ref, s1, s2, s3, s0, m1, m2, m3, root, sems
):
    waves = m1.shape[0]
    moved = ((m3_hbm, m3, s3), (root_hbm, root, s0), (m2_hbm, m2, s2), (m1_hbm, m1, s1))
    chunks = [(source, 0, waves) for source in range(3)]
    size = waves // math.gcd(waves, 4)
    chunks += [(3, first, size) for first in range(0, waves, size)]
    moves = []
    for place, (source, first, size) in enumerate(chunks):
        src, dst, _ = moved[source]
        moves.append(
            pltpu.make_async_copy(src.at[pl.ds(first, size)], dst.at[pl.ds(first, size)], sems.at[place])
        )
        moves[-1].start()
    slots_of(iface_ref, inv_ref)
    for move, (source, first, size) in zip(moves, chunks):
        _, whole_ref, parts_ref = moved[source]
        move.wait()

        def part(wave, carry, whole_ref=whole_ref, parts_ref=parts_ref):
            for node in range(whole_ref.shape[1]):
                parts_ref[wave, node, 0], parts_ref[wave, node, 1] = split(whole_ref[wave, node])
            return carry

        lax.fori_loop(first, first + size, part, 0, unroll=max(1, 4 // whole_ref.shape[1]))


def matvecs(vectors, matrices, flipped):
    row = lax.broadcasted_iota(jnp.int32, (SUB, LANES), 0)
    results = []
    for one in range(0, len(vectors), 2):
        both = first = jnp.zeros((SUB, LANES), F32)
        for place, vector in enumerate(vectors[one : one + 2]):
            high = vector.astype(BF16).astype(F32)
            first = jnp.where(row == 2 * place, high, first)
            both = jnp.where(row == 2 * place, high, jnp.where(row == 2 * place + 1, vector - high, both))
        left = jnp.concatenate([both, first], axis=1).astype(BF16)
        parts = matrices[one : one + 2]
        axis = 1 if flipped else 0
        right = jnp.concatenate([jnp.concatenate([part[0], part[1]], axis=axis) for part in parts], axis=1 - axis)
        out = lax.dot_general(left, right, (((1,), (axis,)), ((), ())), preferred_element_type=F32)
        for place in range(len(parts)):
            mine = out[:, place * LANES : (place + 1) * LANES]
            results.append(mine[2 * place : 2 * place + 1] + mine[2 * place + 1 : 2 * place + 2])
    return results


def up_kernel(
    offsets, rows, me_ref, mine_ref, recv_ref, table_ref, edge_ref, sigma_ref, dif_ref, m1, m2, m3,
    s3_ref, keep_ref, q, edges, pairs, spectrum,
):
    waves, nodes = m1.shape[:2]
    count = len(offsets)
    me = me_ref[0]
    block_rows = 2 * rows + 3 * SUB
    for place, offset in enumerate(offsets):
        source = mine_ref if place < count // 2 else recv_ref
        base = (place % (count // 2)) * block_rows
        for half in range(2):
            q[pl.ds(place * rows, rows), pl.ds(half * 2 * LANES, 2 * LANES)] = source[
                pl.ds(base + half * rows, rows), :
            ]
        edges[me ^ offset] = source[pl.ds(base + 2 * rows, 3 * SUB), :]
    wide = jnp.dot(table_ref[...], q[...], precision=EXACT, preferred_element_type=F32)
    for node in range(nodes):
        spectrum[node] = wide[:, node * LANES : (node + 1) * LANES]
    dif = dif_ref[...]
    lam, _ = decay(dif)
    first_of = lambda t, place: edges[t, pl.ds(SUB * place, SUB), pl.ds(0, LANES)]
    last_of = lambda t, place: edges[t, pl.ds(SUB * place, SUB), pl.ds(LANES, LANES)]
    residual = []
    for t in range(count):
        prev, succ = (t - 1) % count, (t + 1) % count
        residual.append(last_of(prev, 0) - lam * first_of(t, 0) + 0.5 * first_of(t, 1) * last_of(prev, 2))
        residual.append(first_of(succ, 0) - lam * last_of(t, 0) - 0.5 * last_of(t, 1) * first_of(succ, 2))

    def edge_step(wave, carry):
        total = edge_ref[wave, pl.ds(0, 1), :] * residual[0]
        for place in range(1, 2 * count):
            total = total + edge_ref[wave, pl.ds(place, 1), :] * residual[place]
        leaf = total / (dif + sigma_ref[pl.ds(wave, 1), :])
        pairs[wave] = leaf + pltpu.roll(leaf, SUB - 1, 0)
        return carry

    lax.fori_loop(0, waves, edge_step, 0, unroll=4)
    group = math.gcd(waves, GROUP)

    def group_step(index, carry):
        own = [index * group + inner for inner in range(group)]
        level = [
            spectrum[node, pl.ds(wave, 1), :] + pairs[wave, pl.ds(2 * node, 1), :]
            for wave in own
            for node in range(nodes)
        ]
        at = 0
        for matrices in (m1, m2, m3):
            here = [(wave, node) for wave in own for node in range(matrices.shape[1])]
            level = matvecs(level, [matrices[place] for place in here], True)
            for (wave, node), vector in zip(here, level):
                keep_ref[wave, pl.ds(at + node, 1), :] = vector
            at += matrices.shape[1]
            if matrices.shape[1] > 1:
                level = [level[2 * pair] + level[2 * pair + 1] for pair in range(len(level) // 2)]
        for wave, vector in zip(own, level):
            s3_ref[pl.ds(wave, 1), :] = vector
        return carry

    lax.fori_loop(0, waves // group, group_step, 0)


def down_kernel(s3_ref, other_ref, keep_ref, m1, m2, m3, root, out_ref):
    waves, nodes = m1.shape[:2]
    if out_ref.shape[1] > waves:
        out_ref[...] = jnp.zeros(out_ref.shape, F32)
    group = math.gcd(waves, GROUP)

    def group_step(index, carry):
        own = [index * group + inner for inner in range(group)]
        roots = [root[wave, 0] for wave in own]
        level = [s3_ref[pl.ds(wave, 1), :] for wave in own]
        top = matvecs([value + other_ref[pl.ds(wave, 1), :] for wave, value in zip(own, level)], roots, True)
        level = [value - back for value, back in zip(level, matvecs(top, roots, False))]
        at = nodes + nodes // 2
        for matrices in (m3, m2, m1):
            here = [(wave, node) for wave in own for node in range(matrices.shape[1])]
            level = matvecs(level, [matrices[place] for place in here], False)
            if matrices.shape[1] < nodes:
                below = 2 * matrices.shape[1]
                at -= below
                level = [
                    keep_ref[wave, pl.ds(at + 2 * node + child, 1), :] - vector
                    for (wave, node), vector in zip(here, level)
                    for child in range(2)
                ]
        for (wave, node), vector in zip(here, level):
            out_ref[node, pl.ds(wave, 1), :] = vector
        return carry

    lax.fori_loop(0, waves // group, group_step, 0)


def change_of(pairs, count, mine_ref, recv_ref, table_ref, waves):
    nodes = mine_ref.shape[0] * 2 // waves.shape[0]
    wave_rows = waves.shape[0] // count
    for place in range(count):
        source = mine_ref if place < count // 2 else recv_ref
        base = (place % (count // 2)) * nodes * wave_rows
        for at, pair in enumerate(pairs):
            waves[pl.ds(place * wave_rows, wave_rows), pl.ds(at * LANES, LANES)] = source[
                pl.ds(base + pair * wave_rows, wave_rows), :
            ]
    return jnp.dot(table_ref[...], waves[...], precision=EXACT, preferred_element_type=F32)


def pressure_block(planes, block, change, q_ref, inflow_ref, diag_ref, inv_ref):
    rows = q_ref.shape[0]
    start = block * LANES if isinstance(block, int) else pl.multiple_of(block * LANES, LANES)
    row = lax.broadcasted_iota(jnp.int32, (rows, LANES), 0)
    edge_row = lax.broadcasted_iota(jnp.int32, (SUB, LANES), 0)
    lam, _ = decay(diag_ref[pl.ds(block, 1), :])
    left, right, at_first, at_last = (inflow_ref[i, pl.ds(block, 1), :] for i in range(4))
    from_left = at_first + lam * left
    from_right = at_last + lam * right
    local = q_ref[:, pl.ds(start, LANES)]
    value = local + powers(lam, row, planes) * from_left + powers(lam, (planes - 1) - row, planes) * from_right
    span = lam
    for _ in range(int(math.log2(planes))):
        span = span * span
    before = lam * local[0:1] + left + lam * at_first + span * from_right
    after = lam * local[planes - 1 : planes] + right + lam * at_last + span * from_left
    outer = jnp.where(edge_row == 0, before, after)
    slot = inv_ref[pl.ds(block, 1), :]
    taken = slot >= 0
    got = lane_take(change, jnp.broadcast_to(jnp.maximum(slot, 0), change.shape))
    value = jnp.where(taken, 0.5 * value + 0.5 * got[:rows], value)
    return value, jnp.where(taken, 0.5 * outer + 0.5 * got[rows:], outer)


def rim_kernel(
    planes, domains, count, dom_ref, mine_ref, recv_ref, table_ref, q_ref, inflow_ref, diag_ref, inv_ref,
    rim_ref, waves,
):
    nblocks = q_ref.shape[1] // LANES
    for side, block, pair in ((0, nblocks - 1, domains // 2 - 1), (1, 0, 0)):

        @pl.when(dom_ref[0] == side)
        def _(block=block, pair=pair):
            change = change_of((pair,), count, mine_ref, recv_ref, table_ref, waves)
            rim_ref[...] = pressure_block(planes, block, change, q_ref, inflow_ref, diag_ref, inv_ref)[0]


def pressure_kernel(
    planes, domains, count, mine_ref, recv_ref, table_ref, q_ref, inflow_ref, diag_ref, inv_ref,
    ext, change, waves,
):
    rows, cells = q_ref.shape
    nblocks = cells // LANES
    per_pair = 2 * nblocks // domains
    change[...] = change_of(range(domains // 2), count, mine_ref, recv_ref, table_ref, waves)

    def step(block, carry):
        at = column(block // per_pair)
        value, outer = pressure_block(
            planes, block, change[:, pl.ds(at, LANES)], q_ref, inflow_ref, diag_ref, inv_ref
        )
        here = pl.multiple_of((block + 1) * LANES, LANES)
        ext[pl.ds(SUB, rows), pl.ds(here, LANES)] = value
        ext[pl.ds(SUB - 1, 1), pl.ds(here, LANES)] = outer[0:1]
        ext[pl.ds(SUB + planes, 1), pl.ds(here, LANES)] = outer[1:2]
        return carry

    lax.fori_loop(0, nblocks, step, 0, unroll=4)


def corrected_kernel(ext_in, v_ref, halo_ref, sv_ref, fw_ref, nb_ref, p_hbm, out_ref, ext, sems):
    rows, cells = v_ref.shape
    nblocks = cells // LANES
    store = pltpu.make_async_copy(ext_in.at[pl.ds(SUB, rows), pl.ds(LANES, cells)], p_hbm, sems.at[0])
    store.start()
    ext[:, pl.ds(LANES, cells)] = ext_in[:, pl.ds(LANES, cells)]
    ext[pl.ds(SUB, rows), pl.ds(0, LANES)] = halo_ref[...]
    ext[pl.ds(SUB, rows), pl.ds(LANES + cells, LANES)] = halo_ref[...]

    def step(block, carry):
        start = pl.multiple_of(block * LANES, LANES)
        sv = sv_ref[:, pl.ds(start, LANES)]
        _, total = convection(ext, block + 1, block, nblocks, rows, sv, fw_ref, nb_ref)
        out_ref[:, pl.ds(start, LANES)] = v_ref[:, pl.ds(start, LANES)] - total
        return carry

    lax.fori_loop(0, nblocks, step, 0, unroll=4)
    store.wait()


HBM = pl.BlockSpec(memory_space=pltpu.HBM)


def in_hbm(value):
    return pltpu.with_memory_space_constraint(value, pltpu.HBM)


MEBI = 1024 * 1024


def call(kernel, outs, args, scratch=(), specs=None, out_specs=None, aliases=None, limit=8):
    return pl.pallas_call(
        kernel,
        out_shape=[jax.ShapeDtypeStruct(*out) for out in outs],
        in_specs=specs or whole(*args),
        out_specs=out_specs or whole(*outs),
        scratch_shapes=list(scratch),
        compiler_params=pltpu.CompilerParams(vmem_limit_bytes=limit * MEBI),
        input_output_aliases=aliases or {},
    )(*(in_hbm(arg) if spec is HBM else arg for arg, spec in zip(args, specs or whole(*args))))


def inflow(ends, diag, planes):
    count, me = lax.axis_size("span"), lax.axis_index("span")
    lam, _ = decay(diag)
    step = lam
    for _ in range(int(math.log2(planes))):
        step = step * step
    squares = [step]
    while 2 ** len(squares) <= count:
        squares.append(squares[-1] * squares[-1])

    def power(exponent, bits):
        result = jnp.ones_like(step)
        for bit in range(bits):
            result = result * jnp.where((exponent >> bit) & 1 == 1, squares[bit], 1.0)
        return result

    left = jnp.zeros_like(step)
    right = jnp.zeros_like(step)
    ahead, back = ends[0], ends[1]
    bits = int(math.log2(count))
    for bit in range(bits):
        size = 1 << bit
        other = xor_permute(jnp.stack([ahead, back]), "span", size)
        is_right = (me >> bit) & 1 == 1
        place = me & (size - 1)
        reach = power(jnp.where(is_right, place, size - 1 - place), bit)
        left = jnp.where(is_right, left + reach * other[0], left)
        right = jnp.where(is_right, right, right + reach * other[1])
        ahead, back = (
            jnp.where(is_right, ahead + squares[bit] * other[0], other[0] + squares[bit] * ahead),
            jnp.where(is_right, other[1] + squares[bit] * back, back + squares[bit] * other[1]),
        )
    wrap = 1.0 / (1.0 - squares[bits])
    left = left + power(me, bits) * ahead * wrap
    right = right + power(count - 1 - me, bits) * back * wrap
    return left, right


def on_device(
    scalar, span_vel, flux_weight, neighbours, diagonal, interface, schur_one, schur_two, schur_three, schur_root
):
    planes, cells = scalar.shape
    count, me = lax.axis_size("span"), lax.axis_index("span")
    dom = lax.axis_index("dom")
    waves = schur_one.shape[0]
    rows, wave_rows = -(-planes // SUB) * SUB, -(-waves // SUB) * SUB
    nblocks = cells // LANES
    domains, slots = interface.shape
    pair_cells = domains // 2 * slots
    pad = lambda value: value if rows == planes else jnp.pad(value, ((0, rows - planes), (0, 0)))
    field, sv = pad(scalar), pad(span_vel)
    diag = diagonal.reshape(nblocks, LANES)
    offsets = xor_offsets(count)

    def boundary(value):
        edge = jnp.where(dom == 0, value[:, cells - LANES :], value[:, :LANES])
        return xor_permute(edge, "dom", 1)

    block_rows = 2 * rows + 3 * SUB
    vmem = pl.BlockSpec(memory_space=pltpu.VMEM)
    smem = pl.BlockSpec(memory_space=pltpu.SMEM)
    ext_shape = (rows + 2 * SUB, cells + 2 * LANES)
    across = boundary(field)
    local, edge, strip, extended, field_in, sv_in, fw_in, nb_in, diag_in, iface_in = call(
        functools.partial(source_kernel, planes),
        [
            ((rows, cells), F32),
            ((6, nblocks, LANES), F32),
            ((SUB, cells), F32),
            (ext_shape, F32),
            ((rows, cells), F32),
            ((rows, cells), F32),
            (flux_weight.shape, F32),
            (neighbours.shape, jnp.int32),
            ((nblocks, LANES), F32),
            (interface.shape, jnp.int32),
        ],
        (field, sv, flux_weight, neighbours, diag, interface),
        [pltpu.SemaphoreType.DMA((6,))],
        [HBM] * 6,
    )
    local, edge, strip, payload, dif = call(
        functools.partial(seam_kernel, planes),
        [
            ((rows, cells), F32),
            ((6, nblocks, LANES), F32),
            ((SUB, cells), F32),
            ((block_rows, 2 * LANES), F32),
            ((domains, LANES), F32),
        ],
        (dom.reshape(1), across, local, edge, strip, extended, sv_in, fw_in, nb_in, diag_in, iface_in),
        [pltpu.VMEM((rows + 2 * SUB, 3 * LANES), F32)],
        [smem] + [vmem] * 10,
        aliases={2: 0, 3: 1, 4: 2},
    )
    mine, received = gathered(payload, "span")

    in_parts = lambda value: (value.shape[:2] + (2,) + value.shape[2:], BF16)
    slot_of, m1, m2, m3, root = call(
        stage_kernel,
        [
            ((nblocks, LANES), jnp.int32),
            in_parts(schur_one),
            in_parts(schur_two),
            in_parts(schur_three),
            in_parts(schur_root),
        ],
        (iface_in, schur_one, schur_two, schur_three, schur_root),
        [pltpu.VMEM(value.shape, F32) for value in (schur_one, schur_two, schur_three, schur_root)]
        + [pltpu.SemaphoreType.DMA((7,))],
        [vmem] + [HBM] * 4,
        limit=24,
    )
    own_wave = me * waves + jnp.arange(waves, dtype=jnp.int32)
    order = jnp.arange(count, dtype=jnp.int32)
    xored = me ^ (2 * (order % (count // 2)) + order // (count // 2))
    plane_of = xored[:, None] * planes + jnp.arange(rows, dtype=jnp.int32)[None, :]
    valid = jnp.arange(rows) < planes
    table = jnp.where(valid[None, None], fourier_entry(own_wave[:, None, None], plane_of[None]), 0.0)
    table = jnp.pad(table.reshape(waves, count * rows), ((0, wave_rows - waves), (0, 0)))
    edge_planes = (jnp.arange(count)[:, None] * planes + jnp.array([0, planes - 1])[None, :]).reshape(-1)
    edge_table = fourier_entry(own_wave[:, None], edge_planes[None, :].astype(jnp.int32))
    edge_table = jnp.broadcast_to(edge_table[:, :, None], edge_table.shape + (LANES,))
    sigma = jnp.broadcast_to(wave_shift(own_wave)[:, None], (waves, LANES))
    wave_of = xored[:, None] * waves + jnp.arange(wave_rows, dtype=jnp.int32)[None, :]
    row_ids = jnp.arange(rows + SUB, dtype=jnp.int32)
    row_plane = jnp.where(row_ids < rows, row_ids, jnp.where(row_ids == rows, -1, planes))
    row_plane = (me * planes + row_plane + PLANES) % PLANES
    back_table = fourier_entry(wave_of[None], row_plane[:, None, None])
    back_table = jnp.where((jnp.arange(wave_rows) < waves)[None, None], back_table, 0.0)
    back_table = back_table.reshape(rows + SUB, count * wave_rows)
    s3, keep = call(
        functools.partial(up_kernel, offsets, rows),
        [((wave_rows, LANES), F32), ((waves, SUB, LANES), F32)],
        (me.reshape(1), mine, received, table, edge_table, sigma, dif, m1, m2, m3),
        [
            pltpu.VMEM((count * rows, pair_cells), F32),
            pltpu.VMEM((count, 3 * SUB, 2 * LANES), F32),
            pltpu.VMEM((waves, SUB, LANES), F32),
            pltpu.VMEM((pair_cells // LANES, wave_rows, LANES), F32),
        ],
        [smem] + [vmem] * 9,
        limit=16,
    )
    other = xor_permute(s3, "dom", 1)
    (returned,) = call(
        down_kernel, [((pair_cells // LANES, wave_rows, LANES), F32)], (s3, other, keep, m1, m2, m3, root), limit=16
    )
    mine, received = gathered(returned.reshape(-1, LANES), "span")

    up_ring = [(i, (i + 1) % count) for i in range(count)]
    down_ring = [(j, i) for i, j in up_ring]
    q_first, q_last, sv_first, sv_last, v_first, v_last = (edge[i] for i in range(6))
    lam, kappa = decay(diag_in)
    v_before, v_after = lax.ppermute(v_last, "span", up_ring), lax.ppermute(v_first, "span", down_ring)
    at_first = kappa * 0.5 * sv_first * v_before
    at_last = -kappa * 0.5 * sv_last * v_after
    reach = jnp.ones_like(lam)
    for bit in range(int(math.log2(planes))):
        factor = lam
        for _ in range(bit):
            factor = factor * factor
        reach = reach * factor
    ends = jnp.stack([q_last + reach * at_first + at_last, q_first + at_first + reach * at_last])
    left, right = inflow(ends, diag_in, planes)
    flows = jnp.stack([left, right, at_first, at_last])

    wave_scratch = lambda pairs: pltpu.VMEM((count * wave_rows, pairs * LANES), F32)
    parts = (mine, received, back_table, local, flows, diag_in, slot_of)
    (rim,) = call(
        functools.partial(rim_kernel, planes, domains, count),
        [((rows, LANES), F32)],
        (dom.reshape(1),) + parts,
        [wave_scratch(1)],
        [smem] + [vmem] * 7,
    )
    halo = xor_permute(rim, "dom", 1)
    (extended,) = call(
        functools.partial(pressure_kernel, planes, domains, count),
        [(ext_shape, F32)],
        parts,
        [pltpu.VMEM((rows + SUB, pair_cells), F32), wave_scratch(domains // 2)],
    )
    pressure, corrected = call(
        corrected_kernel,
        [((rows, cells), F32), ((rows, cells), F32)],
        (extended, field_in, halo, sv_in, fw_in, nb_in),
        [pltpu.VMEM(ext_shape, F32), pltpu.SemaphoreType.DMA((1,))],
        out_specs=[HBM, vmem],
    )
    return (pressure[:planes], corrected[:planes])


def solution(mesh):
    placed = (
        P(("case", "span"), "dom"),
        P(("case", "span"), "dom"),
        P(None, "dom"),
        P(None, "dom"),
        P("dom"),
        P("dom", None),
        P("span", "dom", None, None),
        P("span", "dom", None, None),
        P("span", "dom", None, None),
        P("span", None, None, None),
    )

    return jax.shard_map(
        on_device,
        mesh=mesh,
        in_specs=placed,
        out_specs=(P(("case", "span"), "dom"), P(("case", "span"), "dom")),
        check_vma=False,
    )
```

```python
import functools
import math

import jax
import jax.numpy as jnp
from jax import lax
from jax.experimental import pallas as pl
from jax.experimental.pallas import tpu as pltpu
from jax.sharding import PartitionSpec as P


PLANES = 128
LANES = 128
SUB = 8
HALF = LANES // 2
GROUP = 8
F32 = jnp.float32
BF16 = jnp.bfloat16
EXACT = lax.Precision.HIGHEST


def fourier_entry(wave_ids, plane_ids):
    middle = PLANES // 2
    wave_num = jnp.where(wave_ids <= middle, wave_ids, wave_ids - middle)
    phase_angle = (wave_num * plane_ids % PLANES).astype(F32) * (2.0 * math.pi / PLANES)
    at_edge = (wave_ids == 0) | (wave_ids == middle)
    weight_row = jnp.where(at_edge, math.sqrt(1.0 / PLANES), math.sqrt(2.0 / PLANES))
    return jnp.where(wave_ids <= middle, jnp.cos(phase_angle), jnp.sin(phase_angle)) * weight_row


def wave_shift(wave_ids):
    middle = PLANES // 2
    wave_num = jnp.where(wave_ids <= middle, wave_ids, wave_ids - middle).astype(F32)
    return (2.0 * jnp.sin(wave_num * (math.pi / PLANES))) ** 2


def xor_permute(value, axis, mask):
    return lax.ppermute(value, axis, [(i, i ^ mask) for i in range(lax.axis_size(axis))])


def gathered(block, axis, apart=False):
    count = lax.axis_size(axis)
    far = [xor_permute(block, axis, mask) for mask in range(count - 2, 0, -2)][::-1]
    if not apart:
        mine = jnp.concatenate([block] + far, axis=0)
        return mine, xor_permute(mine, axis, 1)
    beside = xor_permute(block, axis, 1)
    mine = jnp.concatenate(far, axis=0)
    return block, mine, beside, xor_permute(mine, axis, 1)


def xor_offsets(count):
    return list(range(0, count, 2)) + list(range(1, count, 2))


def whole(*shapes):
    return [pl.BlockSpec(memory_space=pltpu.VMEM) for _ in shapes]


def lane_take(source, index):
    return jnp.take_along_axis(source, index, axis=1, mode="promise_in_bounds")


def decay(diag):
    root = jnp.sqrt(diag + 0.25 * diag * diag)
    return 1.0 / (1.0 + 0.5 * diag + root), 0.5 / root


def powers(base, exponent, limit):
    result = None
    bit, factor = 1, base
    while bit < limit:
        part = jnp.where((exponent & bit) != 0, factor, 1.0)
        result = part if result is None else result * part
        factor = factor * factor
        bit *= 2
    return result


def column(block):
    return block * LANES if isinstance(block, int) else pl.multiple_of(block * LANES, LANES)


def convection(ext, at, block, nblocks, rows, sv, fw_ref, nb_ref):
    start, here = column(block), column(at)
    field = ext[pl.ds(SUB, rows), pl.ds(here, LANES)]
    before = ext[pl.ds(SUB, rows), pl.ds(column(at - 1), LANES)]
    after = ext[pl.ds(SUB, rows), pl.ds(column(at + 1), LANES)]
    lane = lax.broadcasted_iota(jnp.int32, (rows, LANES), 1)
    around = jnp.where(lane < HALF, after, before)
    ahead = ext[pl.ds(SUB + 1, rows), pl.ds(here, LANES)]
    behind = ext[pl.ds(SUB - 1, rows), pl.ds(here, LANES)]
    total = sv * 0.5 * (ahead - behind)
    for slot in range(fw_ref.shape[0]):
        ids = nb_ref[pl.ds(slot, 1), pl.ds(start, LANES)]
        index = jnp.broadcast_to(ids & (LANES - 1), (rows, LANES))
        inside = (((ids >> 7) - block) & (nblocks - 1)) == 0
        near = jnp.where(inside, lane_take(field, index), lane_take(around, index))
        total = total + fw_ref[pl.ds(slot, 1), pl.ds(start, LANES)] * (near - field)
    return field, total


def source_block(planes, ext, at, block, sv_ref, fw_ref, nb_ref, diag_ref, q_ref, edge_ref, strip):
    rows = q_ref.shape[0]
    nblocks = diag_ref.shape[0]
    row = lax.broadcasted_iota(jnp.int32, (rows, LANES), 0)
    start = column(block)
    sv = sv_ref[:, pl.ds(start, LANES)]
    field, total = convection(ext, at, block, nblocks, rows, sv, fw_ref, nb_ref)
    source = field - total
    diag = diag_ref[pl.ds(block, 1), :]
    lam, kappa = decay(diag)
    forward, backward, factor, shift = source, source, lam, 1
    while shift < planes:
        down = jnp.where(row >= shift, pltpu.roll(forward, shift, 0), 0.0)
        up = jnp.where(row < rows - shift, pltpu.roll(backward, rows - shift, 0), 0.0)
        forward = forward + factor * down
        backward = backward + factor * up
        factor, shift = factor * factor, shift * 2
    local = kappa * (forward + (backward - source))
    q_ref[:, pl.ds(start, LANES)] = local
    last = planes - 1
    edges = (
        local[0:1], local[last:planes], sv[0:1], sv[last:planes], field[0:1], field[last:planes], diag,
    )
    for place, value in enumerate(edges):
        strip[pl.ds(place, 1), pl.ds(start, LANES)] = value
        if place < edge_ref.shape[0]:
            edge_ref[place, pl.ds(block, 1), :] = value


def load_kernel(
    dom_ref, v_hbm, sv_hbm, fw_hbm, nb_hbm, diag_hbm, iface_hbm,
    edge_ref, v_ref, sv_ref, fw_ref, nb_ref, diag_ref, iface_ref, sems,
):
    moved = (
        (v_hbm, v_ref), (sv_hbm, sv_ref), (fw_hbm, fw_ref), (nb_hbm, nb_ref), (diag_hbm, diag_ref), (iface_hbm, iface_ref),
    )
    moves = [pltpu.make_async_copy(src, dst, sems.at[i]) for i, (src, dst) in enumerate(moved)]
    for move in moves:
        move.start()
    for move in moves:
        move.wait()
    for side, block in ((0, v_ref.shape[1] // LANES - 1), (1, 0)):

        @pl.when(dom_ref[0] == side)
        def _(block=block):
            edge_ref[...] = v_ref[:, pl.ds(column(block), LANES)]


def source_kernel(
    planes, v_ref, sv_ref, fw_ref, nb_ref, diag_ref, q_ref, edge_ref, strip, ext
):
    rows, cells = v_ref.shape
    nblocks = cells // LANES
    ext[pl.ds(0, SUB), :] = jnp.zeros((SUB, cells + 2 * LANES), F32)
    ext[pl.ds(SUB + rows, SUB), :] = jnp.zeros((SUB, cells + 2 * LANES), F32)
    for side in (0, LANES + cells):
        ext[pl.ds(SUB, rows), pl.ds(side, LANES)] = jnp.zeros((rows, LANES), F32)
    ext[pl.ds(SUB, rows), pl.ds(LANES, cells)] = v_ref[...]

    def step(block, carry):
        source_block(
            planes, ext, block + 1, block, sv_ref, fw_ref, nb_ref, diag_ref, q_ref, edge_ref, strip
        )
        return carry

    lax.fori_loop(0, nblocks, step, 0, unroll=4)


def seam_kernel(
    planes, dom_ref, halo_ref, q_in, edge_in, strip_in, ext, sv_ref, fw_ref, nb_ref, diag_ref, iface_ref,
    q_ref, edge_ref, strip, pay_ref, dif_ref, window,
):
    rows, cells = q_ref.shape
    nblocks = cells // LANES
    for side, block in ((0, nblocks - 1), (1, 0)):

        @pl.when(dom_ref[0] == side)
        def _(side=side, block=block):
            near = side * LANES
            window[:, pl.ds(near, 2 * LANES)] = ext[:, pl.ds(column(block + side), 2 * LANES)]
            window[pl.ds(SUB, rows), pl.ds(2 * LANES * (1 - side), LANES)] = halo_ref[...]
            source_block(
                planes, window, 1, block, sv_ref, fw_ref, nb_ref, diag_ref, q_ref, edge_ref, strip
            )

    domains = iface_ref.shape[0]
    width = cells // domains
    for pair in range(domains // 2):
        total = None
        for domain in (2 * pair, 2 * pair + 1):
            where = iface_ref[pl.ds(domain, 1), :] & (width - 1)
            lane, which = where & (LANES - 1), where >> 7
            inner = jnp.zeros((rows, LANES), F32)
            outer = jnp.zeros((SUB, LANES), F32)
            for part in range(width // LANES):
                start = domain * width + part * LANES
                here = which == part
                index = jnp.broadcast_to(lane, (rows, LANES))
                inner = jnp.where(here, lane_take(q_ref[:, pl.ds(start, LANES)], index), inner)
                index = jnp.broadcast_to(lane, (SUB, LANES))
                outer = jnp.where(here, lane_take(strip[:, pl.ds(start, LANES)], index), outer)
            total = inner if total is None else total + inner
            for place in range(6):
                at = 2 * rows + SUB * (place // 2) + domain
                pay_ref[pl.ds(at, 1), pl.ds((place % 2) * LANES, LANES)] = outer[place : place + 1]
            dif_ref[pl.ds(domain, 1), :] = outer[6:7]
        half, side = divmod(pair, domains // 4)
        pay_ref[pl.ds(half * rows, rows), pl.ds(side * LANES, LANES)] = total


def slots_of(iface_ref, inv_ref):
    domains, slots = iface_ref.shape
    per = inv_ref.shape[0] // domains
    columns = jnp.transpose(jnp.concatenate([iface_ref[...].astype(F32)] * (LANES // domains), axis=0))
    lane = lax.broadcasted_iota(jnp.int32, (slots, LANES), 1)
    slot = lax.broadcasted_iota(jnp.int32, (slots, LANES), 0).astype(F32)
    for domain in range(domains):
        own = columns[:, domain : domain + 1].astype(jnp.int32) & (per * LANES - 1)
        own = jnp.broadcast_to(own, (slots, LANES))
        for part in range(per):
            hit = jnp.where(own == lane + part * LANES, slot, -1.0)
            found = jnp.max(hit, axis=0, keepdims=True)
            inv_ref[pl.ds(domain * per + part, 1), :] = found.astype(jnp.int32)


def split(value):
    high = value.astype(BF16)
    return high, (value - high.astype(F32)).astype(BF16)


def stage_kernel(
    iface_ref, m1_hbm, m2_hbm, m3_hbm, root_hbm, inv_ref, s1, s2, s3, s0, m1, m2, m3, root, sems
):
    waves = m1.shape[0]
    moved = ((m3_hbm, m3, s3), (root_hbm, root, s0), (m2_hbm, m2, s2), (m1_hbm, m1, s1))
    chunks = [(source, 0, waves) for source in range(3)]
    size = waves // math.gcd(waves, 4)
    chunks += [(3, first, size) for first in range(0, waves, size)]
    moves = []
    for place, (source, first, size) in enumerate(chunks):
        src, dst, _ = moved[source]
        moves.append(
            pltpu.make_async_copy(src.at[pl.ds(first, size)], dst.at[pl.ds(first, size)], sems.at[place])
        )
        moves[-1].start()
    slots_of(iface_ref, inv_ref)
    for move, (source, first, size) in zip(moves, chunks):
        _, whole_ref, parts_ref = moved[source]
        move.wait()

        def part(wave, carry, whole_ref=whole_ref, parts_ref=parts_ref):
            for node in range(whole_ref.shape[1]):
                parts_ref[wave, node, 0], parts_ref[wave, node, 1] = split(whole_ref[wave, node])
            return carry

        lax.fori_loop(first, first + size, part, 0, unroll=max(1, 4 // whole_ref.shape[1]))


def matvecs(vectors, matrices, flipped):
    row = lax.broadcasted_iota(jnp.int32, (SUB, LANES), 0)
    results = []
    for one in range(0, len(vectors), 2):
        both = first = jnp.zeros((SUB, LANES), F32)
        for place, vector in enumerate(vectors[one : one + 2]):
            high = vector.astype(BF16).astype(F32)
            first = jnp.where(row == 2 * place, high, first)
            both = jnp.where(row == 2 * place, high, jnp.where(row == 2 * place + 1, vector - high, both))
        left = jnp.concatenate([both, first], axis=1).astype(BF16)
        parts = matrices[one : one + 2]
        axis = 1 if flipped else 0
        right = jnp.concatenate([jnp.concatenate([part[0], part[1]], axis=axis) for part in parts], axis=1 - axis)
        out = lax.dot_general(left, right, (((1,), (axis,)), ((), ())), preferred_element_type=F32)
        for place in range(len(parts)):
            mine = out[:, place * LANES : (place + 1) * LANES]
            results.append(mine[2 * place : 2 * place + 1] + mine[2 * place + 1 : 2 * place + 2])
    return results


def up_kernel(
    offsets, rows, me_ref, own_ref, mine_ref, beside_ref, recv_ref, table_ref, edge_ref, sigma_ref, dif_ref, m1, m2, m3,
    s3_ref, keep_ref, q, edges, pairs, spectrum,
):
    waves, nodes = m1.shape[:2]
    count = len(offsets)
    me = me_ref[0]
    block_rows = 2 * rows + 3 * SUB
    for place, offset in enumerate(offsets):
        side, at = divmod(place, count // 2)
        source = ((own_ref, beside_ref) if at == 0 else (mine_ref, recv_ref))[side]
        base = max(at - 1, 0) * block_rows
        for half in range(2):
            q[pl.ds(place * rows, rows), pl.ds(half * 2 * LANES, 2 * LANES)] = source[
                pl.ds(base + half * rows, rows), :
            ]
        edges[me ^ offset] = source[pl.ds(base + 2 * rows, 3 * SUB), :]
    wide = jnp.dot(table_ref[...], q[...], precision=EXACT, preferred_element_type=F32)
    for node in range(nodes):
        spectrum[node] = wide[:, node * LANES : (node + 1) * LANES]
    dif = dif_ref[...]
    lam, _ = decay(dif)
    first_of = lambda t, place: edges[t, pl.ds(SUB * place, SUB), pl.ds(0, LANES)]
    last_of = lambda t, place: edges[t, pl.ds(SUB * place, SUB), pl.ds(LANES, LANES)]
    residual = []
    for t in range(count):
        prev, succ = (t - 1) % count, (t + 1) % count
        residual.append(last_of(prev, 0) - lam * first_of(t, 0) + 0.5 * first_of(t, 1) * last_of(prev, 2))
        residual.append(first_of(succ, 0) - lam * last_of(t, 0) - 0.5 * last_of(t, 1) * first_of(succ, 2))

    def edge_step(wave, carry):
        total = edge_ref[wave, pl.ds(0, 1), :] * residual[0]
        for place in range(1, 2 * count):
            total = total + edge_ref[wave, pl.ds(place, 1), :] * residual[place]
        leaf = total / (dif + sigma_ref[pl.ds(wave, 1), :])
        pairs[wave] = leaf + pltpu.roll(leaf, SUB - 1, 0)
        return carry

    lax.fori_loop(0, waves, edge_step, 0, unroll=4)
    group = math.gcd(waves, GROUP)

    def group_step(index, carry):
        own = [index * group + inner for inner in range(group)]
        level = [
            spectrum[node, pl.ds(wave, 1), :] + pairs[wave, pl.ds(2 * node, 1), :]
            for wave in own
            for node in range(nodes)
        ]
        at = 0
        for matrices in (m1, m2, m3):
            here = [(wave, node) for wave in own for node in range(matrices.shape[1])]
            level = matvecs(level, [matrices[place] for place in here], True)
            for (wave, node), vector in zip(here, level):
                keep_ref[wave, pl.ds(at + node, 1), :] = vector
            at += matrices.shape[1]
            if matrices.shape[1] > 1:
                level = [level[2 * pair] + level[2 * pair + 1] for pair in range(len(level) // 2)]
        for wave, vector in zip(own, level):
            s3_ref[pl.ds(wave, 1), :] = vector
        return carry

    lax.fori_loop(0, waves // group, group_step, 0)


def down_kernel(s3_ref, other_ref, keep_ref, m1, m2, m3, root, out_ref):
    waves, nodes = m1.shape[:2]
    if out_ref.shape[1] > waves:
        out_ref[...] = jnp.zeros(out_ref.shape, F32)
    group = math.gcd(waves, GROUP)

    def group_step(index, carry):
        own = [index * group + inner for inner in range(group)]
        roots = [root[wave, 0] for wave in own]
        level = [s3_ref[pl.ds(wave, 1), :] for wave in own]
        top = matvecs([value + other_ref[pl.ds(wave, 1), :] for wave, value in zip(own, level)], roots, True)
        level = [value - back for value, back in zip(level, matvecs(top, roots, False))]
        at = nodes + nodes // 2
        for matrices in (m3, m2, m1):
            here = [(wave, node) for wave in own for node in range(matrices.shape[1])]
            level = matvecs(level, [matrices[place] for place in here], False)
            if matrices.shape[1] < nodes:
                below = 2 * matrices.shape[1]
                at -= below
                level = [
                    keep_ref[wave, pl.ds(at + 2 * node + child, 1), :] - vector
                    for (wave, node), vector in zip(here, level)
                    for child in range(2)
                ]
        for (wave, node), vector in zip(here, level):
            out_ref[node, pl.ds(wave, 1), :] = vector
        return carry

    lax.fori_loop(0, waves // group, group_step, 0)


def change_of(pairs, count, blocks, table_ref, waves):
    own_ref, mine_ref, beside_ref, recv_ref = blocks
    wave_rows = waves.shape[0] // count
    for place in range(count):
        side, at = divmod(place, count // 2)
        source = ((own_ref, beside_ref) if at == 0 else (mine_ref, recv_ref))[side]
        base = max(at - 1, 0) * own_ref.shape[0]
        for at, pair in enumerate(pairs):
            waves[pl.ds(place * wave_rows, wave_rows), pl.ds(at * LANES, LANES)] = source[
                pl.ds(base + pair * wave_rows, wave_rows), :
            ]
    return jnp.dot(table_ref[...], waves[...], precision=EXACT, preferred_element_type=F32)


def pressure_block(planes, block, change, q_ref, inflow_ref, diag_ref, inv_ref):
    rows = q_ref.shape[0]
    start = block * LANES if isinstance(block, int) else pl.multiple_of(block * LANES, LANES)
    row = lax.broadcasted_iota(jnp.int32, (rows, LANES), 0)
    edge_row = lax.broadcasted_iota(jnp.int32, (SUB, LANES), 0)
    lam, _ = decay(diag_ref[pl.ds(block, 1), :])
    left, right, at_first, at_last = (inflow_ref[i, pl.ds(block, 1), :] for i in range(4))
    from_left = at_first + lam * left
    from_right = at_last + lam * right
    local = q_ref[:, pl.ds(start, LANES)]
    value = local + powers(lam, row, planes) * from_left + powers(lam, (planes - 1) - row, planes) * from_right
    span = lam
    for _ in range(int(math.log2(planes))):
        span = span * span
    before = lam * local[0:1] + left + lam * at_first + span * from_right
    after = lam * local[planes - 1 : planes] + right + lam * at_last + span * from_left
    outer = jnp.where(edge_row == 0, before, after)
    slot = inv_ref[pl.ds(block, 1), :]
    taken = slot >= 0
    got = lane_take(change, jnp.broadcast_to(jnp.maximum(slot, 0), change.shape))
    value = jnp.where(taken, 0.5 * value + 0.5 * got[:rows], value)
    return value, jnp.where(taken, 0.5 * outer + 0.5 * got[rows:], outer)


def rim_kernel(
    planes, domains, count, dom_ref, own_ref, mine_ref, beside_ref, recv_ref, table_ref, q_ref, inflow_ref, diag_ref, inv_ref,
    rim_ref, waves,
):
    nblocks = q_ref.shape[1] // LANES
    for side, block, pair in ((0, nblocks - 1, domains // 2 - 1), (1, 0, 0)):

        @pl.when(dom_ref[0] == side)
        def _(block=block, pair=pair):
            change = change_of((pair,), count, (own_ref, mine_ref, beside_ref, recv_ref), table_ref, waves)
            rim_ref[...] = pressure_block(planes, block, change, q_ref, inflow_ref, diag_ref, inv_ref)[0]


def pressure_kernel(
    planes, domains, count, own_ref, mine_ref, beside_ref, recv_ref, table_ref, q_ref, inflow_ref, diag_ref, inv_ref,
    ext, change, waves,
):
    rows, cells = q_ref.shape
    nblocks = cells // LANES
    per_pair = 2 * nblocks // domains
    change[...] = change_of(range(domains // 2), count, (own_ref, mine_ref, beside_ref, recv_ref), table_ref, waves)

    def step(block, carry):
        at = column(block // per_pair)
        value, outer = pressure_block(
            planes, block, change[:, pl.ds(at, LANES)], q_ref, inflow_ref, diag_ref, inv_ref
        )
        here = pl.multiple_of((block + 1) * LANES, LANES)
        ext[pl.ds(SUB, rows), pl.ds(here, LANES)] = value
        ext[pl.ds(SUB - 1, 1), pl.ds(here, LANES)] = outer[0:1]
        ext[pl.ds(SUB + planes, 1), pl.ds(here, LANES)] = outer[1:2]
        return carry

    lax.fori_loop(0, nblocks, step, 0, unroll=4)


def corrected_kernel(ext_in, v_ref, halo_ref, sv_ref, fw_ref, nb_ref, p_hbm, out_ref, ext, sems):
    rows, cells = v_ref.shape
    nblocks = cells // LANES
    store = pltpu.make_async_copy(ext_in.at[pl.ds(SUB, rows), pl.ds(LANES, cells)], p_hbm, sems.at[0])
    store.start()
    ext[:, pl.ds(LANES, cells)] = ext_in[:, pl.ds(LANES, cells)]
    ext[pl.ds(SUB, rows), pl.ds(0, LANES)] = halo_ref[...]
    ext[pl.ds(SUB, rows), pl.ds(LANES + cells, LANES)] = halo_ref[...]

    def step(block, carry):
        start = pl.multiple_of(block * LANES, LANES)
        sv = sv_ref[:, pl.ds(start, LANES)]
        _, total = convection(ext, block + 1, block, nblocks, rows, sv, fw_ref, nb_ref)
        out_ref[:, pl.ds(start, LANES)] = v_ref[:, pl.ds(start, LANES)] - total
        return carry

    lax.fori_loop(0, nblocks, step, 0, unroll=4)
    store.wait()


HBM = pl.BlockSpec(memory_space=pltpu.HBM)


def in_hbm(value):
    return pltpu.with_memory_space_constraint(value, pltpu.HBM)


MEBI = 1024 * 1024


def call(kernel, outs, args, scratch=(), specs=None, out_specs=None, aliases=None, limit=8):
    return pl.pallas_call(
        kernel,
        out_shape=[jax.ShapeDtypeStruct(*out) for out in outs],
        in_specs=specs or whole(*args),
        out_specs=out_specs or whole(*outs),
        scratch_shapes=list(scratch),
        compiler_params=pltpu.CompilerParams(vmem_limit_bytes=limit * MEBI),
        input_output_aliases=aliases or {},
    )(*(in_hbm(arg) if spec is HBM else arg for arg, spec in zip(args, specs or whole(*args))))


def inflow(ends, diag, planes):
    count, me = lax.axis_size("span"), lax.axis_index("span")
    lam, _ = decay(diag)
    step = lam
    for _ in range(int(math.log2(planes))):
        step = step * step
    squares = [step]
    while 2 ** len(squares) <= count:
        squares.append(squares[-1] * squares[-1])

    def power(exponent, bits):
        result = jnp.ones_like(step)
        for bit in range(bits):
            result = result * jnp.where((exponent >> bit) & 1 == 1, squares[bit], 1.0)
        return result

    left = jnp.zeros_like(step)
    right = jnp.zeros_like(step)
    ahead, back = ends[0], ends[1]
    bits = int(math.log2(count))
    for bit in range(bits):
        size = 1 << bit
        other = xor_permute(jnp.stack([ahead, back]), "span", size)
        is_right = (me >> bit) & 1 == 1
        place = me & (size - 1)
        reach = power(jnp.where(is_right, place, size - 1 - place), bit)
        left = jnp.where(is_right, left + reach * other[0], left)
        right = jnp.where(is_right, right, right + reach * other[1])
        ahead, back = (
            jnp.where(is_right, ahead + squares[bit] * other[0], other[0] + squares[bit] * ahead),
            jnp.where(is_right, other[1] + squares[bit] * back, back + squares[bit] * other[1]),
        )
    wrap = 1.0 / (1.0 - squares[bits])
    left = left + power(me, bits) * ahead * wrap
    right = right + power(count - 1 - me, bits) * back * wrap
    return left, right


def on_device(
    scalar, span_vel, flux_weight, neighbours, diagonal, interface, schur_one, schur_two, schur_three, schur_root
):
    planes, cells = scalar.shape
    count, me = lax.axis_size("span"), lax.axis_index("span")
    dom = lax.axis_index("dom")
    waves = schur_one.shape[0]
    rows, wave_rows = -(-planes // SUB) * SUB, -(-waves // SUB) * SUB
    nblocks = cells // LANES
    domains, slots = interface.shape
    pair_cells = domains // 2 * slots
    pad = lambda value: value if rows == planes else jnp.pad(value, ((0, rows - planes), (0, 0)))
    field, sv = pad(scalar), pad(span_vel)
    diag = diagonal.reshape(nblocks, LANES)
    offsets = xor_offsets(count)

    block_rows = 2 * rows + 3 * SUB
    vmem = pl.BlockSpec(memory_space=pltpu.VMEM)
    smem = pl.BlockSpec(memory_space=pltpu.SMEM)
    ext_shape = (rows + 2 * SUB, cells + 2 * LANES)
    lent, field_in, sv_in, fw_in, nb_in, diag_in, iface_in = call(
        load_kernel,
        [
            ((rows, LANES), F32),
            ((rows, cells), F32),
            ((rows, cells), F32),
            (flux_weight.shape, F32),
            (neighbours.shape, jnp.int32),
            ((nblocks, LANES), F32),
            (interface.shape, jnp.int32),
        ],
        (dom.reshape(1), field, sv, flux_weight, neighbours, diag, interface),
        [pltpu.SemaphoreType.DMA((6,))],
        [smem] + [HBM] * 6,
    )
    across = xor_permute(lent, "dom", 1)
    local, edge, strip, extended = call(
        functools.partial(source_kernel, planes),
        [
            ((rows, cells), F32),
            ((6, nblocks, LANES), F32),
            ((SUB, cells), F32),
            (ext_shape, F32),
        ],
        (field_in, sv_in, fw_in, nb_in, diag_in),
    )
    local, edge, strip, payload, dif = call(
        functools.partial(seam_kernel, planes),
        [
            ((rows, cells), F32),
            ((6, nblocks, LANES), F32),
            ((SUB, cells), F32),
            ((block_rows, 2 * LANES), F32),
            ((domains, LANES), F32),
        ],
        (dom.reshape(1), across, local, edge, strip, extended, sv_in, fw_in, nb_in, diag_in, iface_in),
        [pltpu.VMEM((rows + 2 * SUB, 3 * LANES), F32)],
        [smem] + [vmem] * 10,
        aliases={2: 0, 3: 1, 4: 2},
    )
    blocks = gathered(payload, "span", apart=True)

    in_parts = lambda value: (value.shape[:2] + (2,) + value.shape[2:], BF16)
    slot_of, m1, m2, m3, root = call(
        stage_kernel,
        [
            ((nblocks, LANES), jnp.int32),
            in_parts(schur_one),
            in_parts(schur_two),
            in_parts(schur_three),
            in_parts(schur_root),
        ],
        (iface_in, schur_one, schur_two, schur_three, schur_root),
        [pltpu.VMEM(value.shape, F32) for value in (schur_one, schur_two, schur_three, schur_root)]
        + [pltpu.SemaphoreType.DMA((7,))],
        [vmem] + [HBM] * 4,
        limit=24,
    )
    own_wave = me * waves + jnp.arange(waves, dtype=jnp.int32)
    order = jnp.arange(count, dtype=jnp.int32)
    xored = me ^ (2 * (order % (count // 2)) + order // (count // 2))
    plane_of = xored[:, None] * planes + jnp.arange(rows, dtype=jnp.int32)[None, :]
    valid = jnp.arange(rows) < planes
    table = jnp.where(valid[None, None], fourier_entry(own_wave[:, None, None], plane_of[None]), 0.0)
    table = jnp.pad(table.reshape(waves, count * rows), ((0, wave_rows - waves), (0, 0)))
    edge_planes = (jnp.arange(count)[:, None] * planes + jnp.array([0, planes - 1])[None, :]).reshape(-1)
    edge_table = fourier_entry(own_wave[:, None], edge_planes[None, :].astype(jnp.int32))
    edge_table = jnp.broadcast_to(edge_table[:, :, None], edge_table.shape + (LANES,))
    sigma = jnp.broadcast_to(wave_shift(own_wave)[:, None], (waves, LANES))
    wave_of = xored[:, None] * waves + jnp.arange(wave_rows, dtype=jnp.int32)[None, :]
    row_ids = jnp.arange(rows + SUB, dtype=jnp.int32)
    row_plane = jnp.where(row_ids < rows, row_ids, jnp.where(row_ids == rows, -1, planes))
    row_plane = (me * planes + row_plane + PLANES) % PLANES
    back_table = fourier_entry(wave_of[None], row_plane[:, None, None])
    back_table = jnp.where((jnp.arange(wave_rows) < waves)[None, None], back_table, 0.0)
    back_table = back_table.reshape(rows + SUB, count * wave_rows)
    s3, keep = call(
        functools.partial(up_kernel, offsets, rows),
        [((wave_rows, LANES), F32), ((waves, SUB, LANES), F32)],
        (me.reshape(1), *blocks, table, edge_table, sigma, dif, m1, m2, m3),
        [
            pltpu.VMEM((count * rows, pair_cells), F32),
            pltpu.VMEM((count, 3 * SUB, 2 * LANES), F32),
            pltpu.VMEM((waves, SUB, LANES), F32),
            pltpu.VMEM((pair_cells // LANES, wave_rows, LANES), F32),
        ],
        [smem] + [vmem] * 11,
        limit=16,
    )
    other = xor_permute(s3, "dom", 1)
    (returned,) = call(
        down_kernel, [((pair_cells // LANES, wave_rows, LANES), F32)], (s3, other, keep, m1, m2, m3, root), limit=16
    )
    blocks = gathered(returned.reshape(-1, LANES), "span", apart=True)

    up_ring = [(i, (i + 1) % count) for i in range(count)]
    down_ring = [(j, i) for i, j in up_ring]
    q_first, q_last, sv_first, sv_last, v_first, v_last = (edge[i] for i in range(6))
    lam, kappa = decay(diag_in)
    v_before, v_after = lax.ppermute(v_last, "span", up_ring), lax.ppermute(v_first, "span", down_ring)
    at_first = kappa * 0.5 * sv_first * v_before
    at_last = -kappa * 0.5 * sv_last * v_after
    reach = jnp.ones_like(lam)
    for bit in range(int(math.log2(planes))):
        factor = lam
        for _ in range(bit):
            factor = factor * factor
        reach = reach * factor
    ends = jnp.stack([q_last + reach * at_first + at_last, q_first + at_first + reach * at_last])
    left, right = inflow(ends, diag_in, planes)
    flows = jnp.stack([left, right, at_first, at_last])

    wave_scratch = lambda pairs: pltpu.VMEM((count * wave_rows, pairs * LANES), F32)
    parts = (*blocks, back_table, local, flows, diag_in, slot_of)
    (rim,) = call(
        functools.partial(rim_kernel, planes, domains, count),
        [((rows, LANES), F32)],
        (dom.reshape(1),) + parts,
        [wave_scratch(1)],
        [smem] + [vmem] * 9,
    )
    halo = xor_permute(rim, "dom", 1)
    (extended,) = call(
        functools.partial(pressure_kernel, planes, domains, count),
        [(ext_shape, F32)],
        parts,
        [pltpu.VMEM((rows + SUB, pair_cells), F32), wave_scratch(domains // 2)],
    )
    pressure, corrected = call(
        corrected_kernel,
        [((rows, cells), F32), ((rows, cells), F32)],
        (extended, field_in, halo, sv_in, fw_in, nb_in),
        [pltpu.VMEM(ext_shape, F32), pltpu.SemaphoreType.DMA((1,))],
        out_specs=[HBM, vmem],
    )
    return (pressure[:planes], corrected[:planes])


def solution(mesh):
    placed = (
        P(("case", "span"), "dom"),
        P(("case", "span"), "dom"),
        P(None, "dom"),
        P(None, "dom"),
        P("dom"),
        P("dom", None),
        P("span", "dom", None, None),
        P("span", "dom", None, None),
        P("span", "dom", None, None),
        P("span", None, None, None),
    )

    return jax.shard_map(
        on_device,
        mesh=mesh,
        in_specs=placed,
        out_specs=(P(("case", "span"), "dom"), P(("case", "span"), "dom")),
        check_vma=False,
    )
```

```python
import functools
import math

import jax
import jax.numpy as jnp
from jax import lax
from jax.experimental import pallas as pl
from jax.experimental.pallas import tpu as pltpu
from jax.sharding import PartitionSpec as P


PLANES = 128
LANES = 128
SUB = 8
HALF = LANES // 2
GROUP = 8
F32 = jnp.float32
BF16 = jnp.bfloat16
EXACT = lax.Precision.HIGHEST


def fourier_entry(wave_ids, plane_ids):
    middle = PLANES // 2
    wave_num = jnp.where(wave_ids <= middle, wave_ids, wave_ids - middle)
    phase_angle = (wave_num * plane_ids % PLANES).astype(F32) * (2.0 * math.pi / PLANES)
    at_edge = (wave_ids == 0) | (wave_ids == middle)
    weight_row = jnp.where(at_edge, math.sqrt(1.0 / PLANES), math.sqrt(2.0 / PLANES))
    return jnp.where(wave_ids <= middle, jnp.cos(phase_angle), jnp.sin(phase_angle)) * weight_row


def wave_shift(wave_ids):
    middle = PLANES // 2
    wave_num = jnp.where(wave_ids <= middle, wave_ids, wave_ids - middle).astype(F32)
    return (2.0 * jnp.sin(wave_num * (math.pi / PLANES))) ** 2


def xor_permute(value, axis, mask):
    return lax.ppermute(value, axis, [(i, i ^ mask) for i in range(lax.axis_size(axis))])


def gathered(block, axis, apart=False):
    count = lax.axis_size(axis)
    far = []
    for mask in range(2, count, 2):
        far.append(xor_permute(block, axis, mask))
    if not apart:
        mine = jnp.concatenate([block] + far, axis=0)
        return mine, xor_permute(mine, axis, 1)
    beside = xor_permute(block, axis, 1)
    mine = jnp.concatenate(far, axis=0)
    return block, mine, beside, xor_permute(mine, axis, 1)


def xor_offsets(count):
    return list(range(0, count, 2)) + list(range(1, count, 2))


def whole(*shapes):
    return [pl.BlockSpec(memory_space=pltpu.VMEM) for _ in shapes]


def lane_take(source, index):
    return jnp.take_along_axis(source, index, axis=1, mode="promise_in_bounds")


def decay(diag):
    root = jnp.sqrt(diag + 0.25 * diag * diag)
    return 1.0 / (1.0 + 0.5 * diag + root), 0.5 / root


def powers(base, exponent, limit):
    result = None
    bit, factor = 1, base
    while bit < limit:
        part = jnp.where((exponent & bit) != 0, factor, 1.0)
        result = part if result is None else result * part
        factor = factor * factor
        bit *= 2
    return result


def column(block):
    return block * LANES if isinstance(block, int) else pl.multiple_of(block * LANES, LANES)


def convection(ext, at, block, nblocks, rows, sv, fw_ref, nb_ref):
    start, here = column(block), column(at)
    field = ext[pl.ds(SUB, rows), pl.ds(here, LANES)]
    before = ext[pl.ds(SUB, rows), pl.ds(column(at - 1), LANES)]
    after = ext[pl.ds(SUB, rows), pl.ds(column(at + 1), LANES)]
    lane = lax.broadcasted_iota(jnp.int32, (rows, LANES), 1)
    around = jnp.where(lane < HALF, after, before)
    ahead = ext[pl.ds(SUB + 1, rows), pl.ds(here, LANES)]
    behind = ext[pl.ds(SUB - 1, rows), pl.ds(here, LANES)]
    total = sv * 0.5 * (ahead - behind)
    for slot in range(fw_ref.shape[0]):
        ids = nb_ref[pl.ds(slot, 1), pl.ds(start, LANES)]
        index = jnp.broadcast_to(ids & (LANES - 1), (rows, LANES))
        inside = (((ids >> 7) - block) & (nblocks - 1)) == 0
        near = jnp.where(inside, lane_take(field, index), lane_take(around, index))
        total = total + fw_ref[pl.ds(slot, 1), pl.ds(start, LANES)] * (near - field)
    return field, total


def source_block(planes, ext, at, block, sv_ref, fw_ref, nb_ref, diag_ref, q_ref, edge_ref, strip):
    rows = q_ref.shape[0]
    nblocks = diag_ref.shape[0]
    row = lax.broadcasted_iota(jnp.int32, (rows, LANES), 0)
    start = column(block)
    sv = sv_ref[:, pl.ds(start, LANES)]
    field, total = convection(ext, at, block, nblocks, rows, sv, fw_ref, nb_ref)
    source = field - total
    diag = diag_ref[pl.ds(block, 1), :]
    lam, kappa = decay(diag)
    forward, backward, factor, shift = source, source, lam, 1
    while shift < planes:
        down = jnp.where(row >= shift, pltpu.roll(forward, shift, 0), 0.0)
        up = jnp.where(row < rows - shift, pltpu.roll(backward, rows - shift, 0), 0.0)
        forward = forward + factor * down
        backward = backward + factor * up
        factor, shift = factor * factor, shift * 2
    local = kappa * (forward + (backward - source))
    q_ref[:, pl.ds(start, LANES)] = local
    last = planes - 1
    edges = (
        local[0:1], local[last:planes], sv[0:1], sv[last:planes], field[0:1], field[last:planes], diag,
    )
    for place, value in enumerate(edges):
        strip[pl.ds(place, 1), pl.ds(start, LANES)] = value
        if place < edge_ref.shape[0]:
            edge_ref[place, pl.ds(block, 1), :] = value


def load_kernel(
    dom_ref, v_hbm, sv_hbm, fw_hbm, nb_hbm, diag_hbm, iface_hbm,
    edge_ref, v_ref, sv_ref, fw_ref, nb_ref, diag_ref, iface_ref, sems,
):
    moved = (
        (v_hbm, v_ref), (sv_hbm, sv_ref), (fw_hbm, fw_ref), (nb_hbm, nb_ref), (diag_hbm, diag_ref), (iface_hbm, iface_ref),
    )
    moves = [pltpu.make_async_copy(src, dst, sems.at[i]) for i, (src, dst) in enumerate(moved)]
    for move in moves:
        move.start()
    for move in moves:
        move.wait()
    for side, block in ((0, v_ref.shape[1] // LANES - 1), (1, 0)):

        @pl.when(dom_ref[0] == side)
        def _(block=block):
            edge_ref[...] = v_ref[:, pl.ds(column(block), LANES)]


def source_kernel(
    planes, v_ref, sv_ref, fw_ref, nb_ref, diag_ref, q_ref, edge_ref, strip, ext
):
    rows, cells = v_ref.shape
    nblocks = cells // LANES
    ext[pl.ds(0, SUB), :] = jnp.zeros((SUB, cells + 2 * LANES), F32)
    ext[pl.ds(SUB + rows, SUB), :] = jnp.zeros((SUB, cells + 2 * LANES), F32)
    for side in (0, LANES + cells):
        ext[pl.ds(SUB, rows), pl.ds(side, LANES)] = jnp.zeros((rows, LANES), F32)
    ext[pl.ds(SUB, rows), pl.ds(LANES, cells)] = v_ref[...]

    def step(block, carry):
        source_block(
            planes, ext, block + 1, block, sv_ref, fw_ref, nb_ref, diag_ref, q_ref, edge_ref, strip
        )
        return carry

    lax.fori_loop(0, nblocks, step, 0, unroll=4)


def seam_kernel(
    planes, dom_ref, halo_ref, q_in, edge_in, strip_in, ext, sv_ref, fw_ref, nb_ref, diag_ref, iface_ref,
    q_ref, edge_ref, pay_ref, dif_ref, window, strip,
):
    rows, cells = q_ref.shape
    nblocks = cells // LANES
    q_ref[...] = q_in[...]
    edge_ref[...] = edge_in[...]
    strip[...] = strip_in[...]
    for side, block in ((0, nblocks - 1), (1, 0)):

        @pl.when(dom_ref[0] == side)
        def _(side=side, block=block):
            near = side * LANES
            window[:, pl.ds(near, 2 * LANES)] = ext[:, pl.ds(column(block + side), 2 * LANES)]
            window[pl.ds(SUB, rows), pl.ds(2 * LANES * (1 - side), LANES)] = halo_ref[...]
            source_block(
                planes, window, 1, block, sv_ref, fw_ref, nb_ref, diag_ref, q_ref, edge_ref, strip
            )

    domains = iface_ref.shape[0]
    width = cells // domains
    for pair in range(domains // 2):
        total = None
        for domain in (2 * pair, 2 * pair + 1):
            where = iface_ref[pl.ds(domain, 1), :] & (width - 1)
            lane, which = where & (LANES - 1), where >> 7
            inner = jnp.zeros((rows, LANES), F32)
            outer = jnp.zeros((SUB, LANES), F32)
            for part in range(width // LANES):
                start = domain * width + part * LANES
                here = which == part
                index = jnp.broadcast_to(lane, (rows, LANES))
                inner = jnp.where(here, lane_take(q_ref[:, pl.ds(start, LANES)], index), inner)
                index = jnp.broadcast_to(lane, (SUB, LANES))
                outer = jnp.where(here, lane_take(strip[:, pl.ds(start, LANES)], index), outer)
            total = inner if total is None else total + inner
            for place in range(6):
                at = 2 * rows + SUB * (place // 2) + domain
                pay_ref[pl.ds(at, 1), pl.ds((place % 2) * LANES, LANES)] = outer[place : place + 1]
            dif_ref[pl.ds(domain, 1), :] = outer[6:7]
        half, side = divmod(pair, domains // 4)
        pay_ref[pl.ds(half * rows, rows), pl.ds(side * LANES, LANES)] = total


def slots_of(iface_ref, inv_ref):
    domains, slots = iface_ref.shape
    per = inv_ref.shape[0] // domains
    columns = jnp.transpose(jnp.concatenate([iface_ref[...].astype(F32)] * (LANES // domains), axis=0))
    lane = lax.broadcasted_iota(jnp.int32, (slots, LANES), 1)
    slot = lax.broadcasted_iota(jnp.int32, (slots, LANES), 0).astype(F32)
    for domain in range(domains):
        own = columns[:, domain : domain + 1].astype(jnp.int32) & (per * LANES - 1)
        own = jnp.broadcast_to(own, (slots, LANES))
        for part in range(per):
            hit = jnp.where(own == lane + part * LANES, slot, -1.0)
            found = jnp.max(hit, axis=0, keepdims=True)
            inv_ref[pl.ds(domain * per + part, 1), :] = found.astype(jnp.int32)


def split(value):
    high = value.astype(BF16)
    return high, (value - high.astype(F32)).astype(BF16)


def stage_kernel(
    iface_ref, m1_hbm, m2_hbm, m3_hbm, root_hbm, inv_ref, s1, s2, s3, s0, m1, m2, m3, root, sems
):
    waves = m1.shape[0]
    moved = ((m3_hbm, m3, s3), (root_hbm, root, s0), (m2_hbm, m2, s2), (m1_hbm, m1, s1))
    chunks = [(source, 0, waves) for source in range(3)]
    size = waves // math.gcd(waves, 4)
    chunks += [(3, first, size) for first in range(0, waves, size)]
    moves = []
    for place, (source, first, size) in enumerate(chunks):
        src, dst, _ = moved[source]
        moves.append(
            pltpu.make_async_copy(src.at[pl.ds(first, size)], dst.at[pl.ds(first, size)], sems.at[place])
        )
        moves[-1].start()
    slots_of(iface_ref, inv_ref)
    for move, (source, first, size) in zip(moves, chunks):
        _, whole_ref, parts_ref = moved[source]
        move.wait()

        def part(wave, carry, whole_ref=whole_ref, parts_ref=parts_ref):
            for node in range(whole_ref.shape[1]):
                parts_ref[wave, node, 0], parts_ref[wave, node, 1] = split(whole_ref[wave, node])
            return carry

        lax.fori_loop(first, first + size, part, 0, unroll=max(1, 4 // whole_ref.shape[1]))


def matvecs(vectors, matrices, flipped):
    row = lax.broadcasted_iota(jnp.int32, (SUB, LANES), 0)
    results = []
    for one in range(0, len(vectors), 2):
        both = first = jnp.zeros((SUB, LANES), F32)
        for place, vector in enumerate(vectors[one : one + 2]):
            high = vector.astype(BF16).astype(F32)
            first = jnp.where(row == 2 * place, high, first)
            both = jnp.where(row == 2 * place, high, jnp.where(row == 2 * place + 1, vector - high, both))
        left = jnp.concatenate([both, first], axis=1).astype(BF16)
        parts = matrices[one : one + 2]
        axis = 1 if flipped else 0
        right = jnp.concatenate([jnp.concatenate([part[0], part[1]], axis=axis) for part in parts], axis=1 - axis)
        out = lax.dot_general(left, right, (((1,), (axis,)), ((), ())), preferred_element_type=F32)
        for place in range(len(parts)):
            mine = out[:, place * LANES : (place + 1) * LANES]
            results.append(mine[2 * place : 2 * place + 1] + mine[2 * place + 1 : 2 * place + 2])
    return results


def up_kernel(
    offsets, rows, me_ref, own_ref, mine_ref, beside_ref, recv_ref, table_ref, edge_ref, sigma_ref, dif_ref, m1, m2, m3,
    s3_ref, keep_ref, q, edges, pairs, spectrum,
):
    waves, nodes = m1.shape[:2]
    count = len(offsets)
    me = me_ref[0]
    block_rows = 2 * rows + 3 * SUB
    for place, offset in enumerate(offsets):
        side, at = divmod(place, count // 2)
        source = ((own_ref, beside_ref) if at == 0 else (mine_ref, recv_ref))[side]
        base = max(at - 1, 0) * block_rows
        for half in range(2):
            q[pl.ds(place * rows, rows), pl.ds(half * 2 * LANES, 2 * LANES)] = source[
                pl.ds(base + half * rows, rows), :
            ]
        edges[me ^ offset] = source[pl.ds(base + 2 * rows, 3 * SUB), :]
    wide = jnp.dot(table_ref[...], q[...], precision=EXACT, preferred_element_type=F32)
    for node in range(nodes):
        spectrum[node] = wide[:, node * LANES : (node + 1) * LANES]
    dif = dif_ref[...]
    lam, _ = decay(dif)
    first_of = lambda t, place: edges[t, pl.ds(SUB * place, SUB), pl.ds(0, LANES)]
    last_of = lambda t, place: edges[t, pl.ds(SUB * place, SUB), pl.ds(LANES, LANES)]
    residual = []
    for t in range(count):
        prev, succ = (t - 1) % count, (t + 1) % count
        residual.append(last_of(prev, 0) - lam * first_of(t, 0) + 0.5 * first_of(t, 1) * last_of(prev, 2))
        residual.append(first_of(succ, 0) - lam * last_of(t, 0) - 0.5 * last_of(t, 1) * first_of(succ, 2))

    def edge_step(wave, carry):
        total = edge_ref[wave, pl.ds(0, 1), :] * residual[0]
        for place in range(1, 2 * count):
            total = total + edge_ref[wave, pl.ds(place, 1), :] * residual[place]
        leaf = total / (dif + sigma_ref[pl.ds(wave, 1), :])
        pairs[wave] = leaf + pltpu.roll(leaf, SUB - 1, 0)
        return carry

    lax.fori_loop(0, waves, edge_step, 0, unroll=4)
    group = math.gcd(waves, GROUP)

    def group_step(index, carry):
        own = [index * group + inner for inner in range(group)]
        level = [
            spectrum[node, pl.ds(wave, 1), :] + pairs[wave, pl.ds(2 * node, 1), :]
            for wave in own
            for node in range(nodes)
        ]
        at = 0
        for matrices in (m1, m2, m3):
            here = [(wave, node) for wave in own for node in range(matrices.shape[1])]
            level = matvecs(level, [matrices[place] for place in here], True)
            for (wave, node), vector in zip(here, level):
                keep_ref[wave, pl.ds(at + node, 1), :] = vector
            at += matrices.shape[1]
            if matrices.shape[1] > 1:
                level = [level[2 * pair] + level[2 * pair + 1] for pair in range(len(level) // 2)]
        for wave, vector in zip(own, level):
            s3_ref[pl.ds(wave, 1), :] = vector
        return carry

    lax.fori_loop(0, waves // group, group_step, 0)


def down_kernel(s3_ref, other_ref, keep_ref, m1, m2, m3, root, out_ref):
    waves, nodes = m1.shape[:2]
    if out_ref.shape[1] > waves:
        out_ref[...] = jnp.zeros(out_ref.shape, F32)
    group = math.gcd(waves, GROUP)

    def group_step(index, carry):
        own = [index * group + inner for inner in range(group)]
        roots = [root[wave, 0] for wave in own]
        level = [s3_ref[pl.ds(wave, 1), :] for wave in own]
        top = matvecs([value + other_ref[pl.ds(wave, 1), :] for wave, value in zip(own, level)], roots, True)
        level = [value - back for value, back in zip(level, matvecs(top, roots, False))]
        at = nodes + nodes // 2
        for matrices in (m3, m2, m1):
            here = [(wave, node) for wave in own for node in range(matrices.shape[1])]
            level = matvecs(level, [matrices[place] for place in here], False)
            if matrices.shape[1] < nodes:
                below = 2 * matrices.shape[1]
                at -= below
                level = [
                    keep_ref[wave, pl.ds(at + 2 * node + child, 1), :] - vector
                    for (wave, node), vector in zip(here, level)
                    for child in range(2)
                ]
        for (wave, node), vector in zip(here, level):
            out_ref[node, pl.ds(wave, 1), :] = vector
        return carry

    lax.fori_loop(0, waves // group, group_step, 0)


def change_of(pairs, count, blocks, table_ref, waves):
    own_ref, mine_ref, beside_ref, recv_ref = blocks
    wave_rows = waves.shape[0] // count
    for place in range(count):
        side, at = divmod(place, count // 2)
        source = ((own_ref, beside_ref) if at == 0 else (mine_ref, recv_ref))[side]
        base = max(at - 1, 0) * own_ref.shape[0]
        for at, pair in enumerate(pairs):
            waves[pl.ds(place * wave_rows, wave_rows), pl.ds(at * LANES, LANES)] = source[
                pl.ds(base + pair * wave_rows, wave_rows), :
            ]
    return jnp.dot(table_ref[...], waves[...], precision=EXACT, preferred_element_type=F32)


def pressure_block(planes, block, change, q_ref, inflow_ref, diag_ref, inv_ref):
    rows = q_ref.shape[0]
    start = block * LANES if isinstance(block, int) else pl.multiple_of(block * LANES, LANES)
    row = lax.broadcasted_iota(jnp.int32, (rows, LANES), 0)
    edge_row = lax.broadcasted_iota(jnp.int32, (SUB, LANES), 0)
    lam, _ = decay(diag_ref[pl.ds(block, 1), :])
    left, right, at_first, at_last = (inflow_ref[i, pl.ds(block, 1), :] for i in range(4))
    from_left = at_first + lam * left
    from_right = at_last + lam * right
    local = q_ref[:, pl.ds(start, LANES)]
    value = local + powers(lam, row, planes) * from_left + powers(lam, (planes - 1) - row, planes) * from_right
    span = lam
    for _ in range(int(math.log2(planes))):
        span = span * span
    before = lam * local[0:1] + left + lam * at_first + span * from_right
    after = lam * local[planes - 1 : planes] + right + lam * at_last + span * from_left
    outer = jnp.where(edge_row == 0, before, after)
    slot = inv_ref[pl.ds(block, 1), :]
    taken = slot >= 0
    got = lane_take(change, jnp.broadcast_to(jnp.maximum(slot, 0), change.shape))
    value = jnp.where(taken, 0.5 * value + 0.5 * got[:rows], value)
    return value, jnp.where(taken, 0.5 * outer + 0.5 * got[rows:], outer)


def rim_kernel(
    planes, domains, count, dom_ref, own_ref, mine_ref, beside_ref, recv_ref, table_ref, q_ref, inflow_ref, diag_ref, inv_ref,
    rim_ref, waves,
):
    nblocks = q_ref.shape[1] // LANES
    for side, block, pair in ((0, nblocks - 1, domains // 2 - 1), (1, 0, 0)):

        @pl.when(dom_ref[0] == side)
        def _(block=block, pair=pair):
            change = change_of((pair,), count, (own_ref, mine_ref, beside_ref, recv_ref), table_ref, waves)
            rim_ref[...] = pressure_block(planes, block, change, q_ref, inflow_ref, diag_ref, inv_ref)[0]


def pressure_kernel(
    planes, domains, count, own_ref, mine_ref, beside_ref, recv_ref, table_ref, q_ref, inflow_ref, diag_ref, inv_ref,
    ext, change, waves,
):
    rows, cells = q_ref.shape
    nblocks = cells // LANES
    per_pair = 2 * nblocks // domains
    change[...] = change_of(range(domains // 2), count, (own_ref, mine_ref, beside_ref, recv_ref), table_ref, waves)

    def step(block, carry):
        at = column(block // per_pair)
        value, outer = pressure_block(
            planes, block, change[:, pl.ds(at, LANES)], q_ref, inflow_ref, diag_ref, inv_ref
        )
        here = pl.multiple_of((block + 1) * LANES, LANES)
        ext[pl.ds(SUB, rows), pl.ds(here, LANES)] = value
        ext[pl.ds(SUB - 1, 1), pl.ds(here, LANES)] = outer[0:1]
        ext[pl.ds(SUB + planes, 1), pl.ds(here, LANES)] = outer[1:2]
        return carry

    lax.fori_loop(0, nblocks, step, 0, unroll=4)


def corrected_kernel(ext_in, v_ref, halo_ref, sv_ref, fw_ref, nb_ref, p_hbm, out_ref, ext, sems):
    rows, cells = v_ref.shape
    nblocks = cells // LANES
    store = pltpu.make_async_copy(ext_in.at[pl.ds(SUB, rows), pl.ds(LANES, cells)], p_hbm, sems.at[0])
    store.start()
    ext[:, pl.ds(LANES, cells)] = ext_in[:, pl.ds(LANES, cells)]
    ext[pl.ds(SUB, rows), pl.ds(0, LANES)] = halo_ref[...]
    ext[pl.ds(SUB, rows), pl.ds(LANES + cells, LANES)] = halo_ref[...]

    def step(block, carry):
        start = pl.multiple_of(block * LANES, LANES)
        sv = sv_ref[:, pl.ds(start, LANES)]
        _, total = convection(ext, block + 1, block, nblocks, rows, sv, fw_ref, nb_ref)
        out_ref[:, pl.ds(start, LANES)] = v_ref[:, pl.ds(start, LANES)] - total
        return carry

    lax.fori_loop(0, nblocks, step, 0, unroll=4)
    store.wait()


HBM = pl.BlockSpec(memory_space=pltpu.HBM)


def in_hbm(value):
    return pltpu.with_memory_space_constraint(value, pltpu.HBM)


MEBI = 1024 * 1024


def call(kernel, outs, args, scratch=(), specs=None, out_specs=None, limit=8):
    return pl.pallas_call(
        kernel,
        out_shape=[jax.ShapeDtypeStruct(*out) for out in outs],
        in_specs=specs or whole(*args),
        out_specs=out_specs or whole(*outs),
        scratch_shapes=list(scratch),
        compiler_params=pltpu.CompilerParams(vmem_limit_bytes=limit * MEBI),
    )(*(in_hbm(arg) if spec is HBM else arg for arg, spec in zip(args, specs or whole(*args))))


def inflow(ends, diag, planes):
    count, me = lax.axis_size("span"), lax.axis_index("span")
    lam, _ = decay(diag)
    step = lam
    for _ in range(int(math.log2(planes))):
        step = step * step
    squares = [step]
    while 2 ** len(squares) <= count:
        squares.append(squares[-1] * squares[-1])

    def power(exponent, bits):
        result = jnp.ones_like(step)
        for bit in range(bits):
            result = result * jnp.where((exponent >> bit) & 1 == 1, squares[bit], 1.0)
        return result

    left = jnp.zeros_like(step)
    right = jnp.zeros_like(step)
    ahead, back = ends[0], ends[1]
    bits = int(math.log2(count))
    for bit in range(bits):
        size = 1 << bit
        other = xor_permute(jnp.stack([ahead, back]), "span", size)
        is_right = (me >> bit) & 1 == 1
        place = me & (size - 1)
        reach = power(jnp.where(is_right, place, size - 1 - place), bit)
        left = jnp.where(is_right, left + reach * other[0], left)
        right = jnp.where(is_right, right, right + reach * other[1])
        ahead, back = (
            jnp.where(is_right, ahead + squares[bit] * other[0], other[0] + squares[bit] * ahead),
            jnp.where(is_right, other[1] + squares[bit] * back, back + squares[bit] * other[1]),
        )
    wrap = 1.0 / (1.0 - squares[bits])
    left = left + power(me, bits) * ahead * wrap
    right = right + power(count - 1 - me, bits) * back * wrap
    return left, right


def on_device(
    scalar, span_vel, flux_weight, neighbours, diagonal, interface, schur_one, schur_two, schur_three, schur_root
):
    planes, cells = scalar.shape
    count, me = lax.axis_size("span"), lax.axis_index("span")
    dom = lax.axis_index("dom")
    waves = schur_one.shape[0]
    rows, wave_rows = -(-planes // SUB) * SUB, -(-waves // SUB) * SUB
    nblocks = cells // LANES
    domains, slots = interface.shape
    pair_cells = domains // 2 * slots
    pad = lambda value: value if rows == planes else jnp.pad(value, ((0, rows - planes), (0, 0)))
    field, sv = pad(scalar), pad(span_vel)
    diag = diagonal.reshape(nblocks, LANES)
    offsets = xor_offsets(count)

    block_rows = 2 * rows + 3 * SUB
    vmem = pl.BlockSpec(memory_space=pltpu.VMEM)
    smem = pl.BlockSpec(memory_space=pltpu.SMEM)
    ext_shape = (rows + 2 * SUB, cells + 2 * LANES)
    lent, field_in, sv_in, fw_in, nb_in, diag_in, iface_in = call(
        load_kernel,
        [
            ((rows, LANES), F32),
            ((rows, cells), F32),
            ((rows, cells), F32),
            (flux_weight.shape, F32),
            (neighbours.shape, jnp.int32),
            ((nblocks, LANES), F32),
            (interface.shape, jnp.int32),
        ],
        (dom.reshape(1), field, sv, flux_weight, neighbours, diag, interface),
        [pltpu.SemaphoreType.DMA((6,))],
        [smem] + [HBM] * 6,
    )
    across = xor_permute(lent, "dom", 1)
    local, edge, strip, extended = call(
        functools.partial(source_kernel, planes),
        [
            ((rows, cells), F32),
            ((6, nblocks, LANES), F32),
            ((SUB, cells), F32),
            (ext_shape, F32),
        ],
        (field_in, sv_in, fw_in, nb_in, diag_in),
    )
    local, edge, payload, dif = call(
        functools.partial(seam_kernel, planes),
        [
            ((rows, cells), F32),
            ((6, nblocks, LANES), F32),
            ((block_rows, 2 * LANES), F32),
            ((domains, LANES), F32),
        ],
        (dom.reshape(1), across, local, edge, strip, extended, sv_in, fw_in, nb_in, diag_in, iface_in),
        [pltpu.VMEM((rows + 2 * SUB, 3 * LANES), F32), pltpu.VMEM((SUB, cells), F32)],
        [smem] + [vmem] * 10,
    )
    blocks = gathered(payload, "span", apart=True)

    in_parts = lambda value: (value.shape[:2] + (2,) + value.shape[2:], BF16)
    slot_of, m1, m2, m3, root = call(
        stage_kernel,
        [
            ((nblocks, LANES), jnp.int32),
            in_parts(schur_one),
            in_parts(schur_two),
            in_parts(schur_three),
            in_parts(schur_root),
        ],
        (iface_in, schur_one, schur_two, schur_three, schur_root),
        [pltpu.VMEM(value.shape, F32) for value in (schur_one, schur_two, schur_three, schur_root)]
        + [pltpu.SemaphoreType.DMA((7,))],
        [vmem] + [HBM] * 4,
        limit=24,
    )
    own_wave = me * waves + jnp.arange(waves, dtype=jnp.int32)
    order = jnp.arange(count, dtype=jnp.int32)
    xored = me ^ (2 * (order % (count // 2)) + order // (count // 2))
    plane_of = xored[:, None] * planes + jnp.arange(rows, dtype=jnp.int32)[None, :]
    valid = jnp.arange(rows) < planes
    table = jnp.where(valid[None, None], fourier_entry(own_wave[:, None, None], plane_of[None]), 0.0)
    table = jnp.pad(table.reshape(waves, count * rows), ((0, wave_rows - waves), (0, 0)))
    edge_planes = (jnp.arange(count)[:, None] * planes + jnp.array([0, planes - 1])[None, :]).reshape(-1)
    edge_table = fourier_entry(own_wave[:, None], edge_planes[None, :].astype(jnp.int32))
    edge_table = jnp.broadcast_to(edge_table[:, :, None], edge_table.shape + (LANES,))
    sigma = jnp.broadcast_to(wave_shift(own_wave)[:, None], (waves, LANES))
    wave_of = xored[:, None] * waves + jnp.arange(wave_rows, dtype=jnp.int32)[None, :]
    row_ids = jnp.arange(rows + SUB, dtype=jnp.int32)
    row_plane = jnp.where(row_ids < rows, row_ids, jnp.where(row_ids == rows, -1, planes))
    row_plane = (me * planes + row_plane + PLANES) % PLANES
    back_table = fourier_entry(wave_of[None], row_plane[:, None, None])
    back_table = jnp.where((jnp.arange(wave_rows) < waves)[None, None], back_table, 0.0)
    back_table = back_table.reshape(rows + SUB, count * wave_rows)
    s3, keep = call(
        functools.partial(up_kernel, offsets, rows),
        [((wave_rows, LANES), F32), ((waves, SUB, LANES), F32)],
        (me.reshape(1), *blocks, table, edge_table, sigma, dif, m1, m2, m3),
        [
            pltpu.VMEM((count * rows, pair_cells), F32),
            pltpu.VMEM((count, 3 * SUB, 2 * LANES), F32),
            pltpu.VMEM((waves, SUB, LANES), F32),
            pltpu.VMEM((pair_cells // LANES, wave_rows, LANES), F32),
        ],
        [smem] + [vmem] * 11,
        limit=16,
    )
    other = xor_permute(s3, "dom", 1)
    (returned,) = call(
        down_kernel, [((pair_cells // LANES, wave_rows, LANES), F32)], (s3, other, keep, m1, m2, m3, root), limit=16
    )
    blocks = gathered(returned.reshape(-1, LANES), "span", apart=True)

    up_ring = [(i, (i + 1) % count) for i in range(count)]
    down_ring = [(j, i) for i, j in up_ring]
    q_first, q_last, sv_first, sv_last, v_first, v_last = (edge[i] for i in range(6))
    lam, kappa = decay(diag_in)
    v_before, v_after = lax.ppermute(v_last, "span", up_ring), lax.ppermute(v_first, "span", down_ring)
    at_first = kappa * 0.5 * sv_first * v_before
    at_last = -kappa * 0.5 * sv_last * v_after
    reach = jnp.ones_like(lam)
    for bit in range(int(math.log2(planes))):
        factor = lam
        for _ in range(bit):
            factor = factor * factor
        reach = reach * factor
    ends = jnp.stack([q_last + reach * at_first + at_last, q_first + at_first + reach * at_last])
    left, right = inflow(ends, diag_in, planes)
    flows = jnp.stack([left, right, at_first, at_last])

    wave_scratch = lambda pairs: pltpu.VMEM((count * wave_rows, pairs * LANES), F32)
    parts = (*blocks, back_table, local, flows, diag_in, slot_of)
    (rim,) = call(
        functools.partial(rim_kernel, planes, domains, count),
        [((rows, LANES), F32)],
        (dom.reshape(1),) + parts,
        [wave_scratch(1)],
        [smem] + [vmem] * 9,
    )
    halo = xor_permute(rim, "dom", 1)
    (extended,) = call(
        functools.partial(pressure_kernel, planes, domains, count),
        [(ext_shape, F32)],
        parts,
        [pltpu.VMEM((rows + SUB, pair_cells), F32), wave_scratch(domains // 2)],
    )
    pressure, corrected = call(
        corrected_kernel,
        [((rows, cells), F32), ((rows, cells), F32)],
        (extended, field_in, halo, sv_in, fw_in, nb_in),
        [pltpu.VMEM(ext_shape, F32), pltpu.SemaphoreType.DMA((1,))],
        out_specs=[HBM, vmem],
    )
    return (pressure[:planes], corrected[:planes])


def solution(mesh):
    placed = (
        P(("case", "span"), "dom"),
        P(("case", "span"), "dom"),
        P(None, "dom"),
        P(None, "dom"),
        P("dom"),
        P("dom", None),
        P("span", "dom", None, None),
        P("span", "dom", None, None),
        P("span", "dom", None, None),
        P("span", None, None, None),
    )

    return jax.shard_map(
        on_device,
        mesh=mesh,
        in_specs=placed,
        out_specs=(P(("case", "span"), "dom"), P(("case", "span"), "dom")),
        check_vma=False,
    )
```
